32 devices in a mesh: grp: 2 (over x), pix: 16 (over z, y, core).
Axes of the slice: x: 2, y: 2, z: 4, core: 2. Of those that a mesh axis runs over, the one named last changes fastest.
Arguments:
- slcs: bfloat16 [2, 2048, 2048], P(None, ('grp', 'pix')), parts along dimension 1, may hold values from -6 to 6
- ref_date: int32 [2], P('grp'), parts along dimension 0, may hold values from 0 to 15
Outputs:
- spectrum: float32 [2, 2048, 2048], P(None, ('grp', 'pix')), parts along dimension 1
- compressed: float32 [2, 64, 4096], P(None, None, ('grp', 'pix')), parts along dimension 2
The draws below stay inside these ranges and needn't reach their ends.
There are 2 independent parts, one for each index of `grp`. The reference program is written for one: setup_inputs(seed, part) draws one part's arguments, and reference() takes and returns one part's arrays. A program takes and returns all parts, laid end to end along the dimension named above; each array names one. Nothing has to cross between parts.
All inputs are finite; a program needn't handle non-finite values.
Results may differ from the reference program's by a relative error of at most 0.0057.
Values may be sent and summed in bfloat16 or wider, within the bound.
No kernel may reach another device: no remote copies, remote signals or barrier semaphores. Data moves between devices by JAX's collectives and lax.ppermute only.
A program may use at most 64 MiB of HBM per device.

```python
import math
import jax
import jax.numpy as jnp
from jax import lax

DATES = 16
ROWS = 64
COLS_DEV = 128
HALF_X = 5
HALF_Y = 2
POWER_ITERS = 6
COLS = 2048
N_PIX = 16


def shard_levels(key, shape, split, smallest, top_value):
    def one(dim, parts):
        draws = jax.random.uniform(jax.random.fold_in(jax.random.fold_in(key, 6), dim), (parts,), jnp.float32, smallest / len(split), top_value / len(split))
        return jnp.repeat(jnp.exp(draws), shape[dim] // parts).reshape((-1,) + (1,) * (len(shape) - dim - 1))

    level = one(*split[0])
    for cut in split[1:]:
        level = level * one(*cut)
    return level


def normal_values(stream_key, shape, deviation, limit, shards=(), kind=jnp.bfloat16):
    entries = deviation * jax.random.normal(stream_key, shape, jnp.float32)
    if shards:
        entries = entries * shard_levels(stream_key, shape, shards, -0.22, 0.18)
    return jnp.clip(entries, -limit, limit).astype(kind)


def setup_inputs(seed: int = 0, part: int = 0) -> dict:
    seeds = jax.random.split(jax.random.key(seed), 3)
    part_keys = jax.random.split(jax.random.fold_in(seeds[2], part), 3)
    return {
        "slcs": normal_values(part_keys[0], (2, DATES * ROWS, COLS), 1.0, 6.0, ((1, 16),)),
        "ref_date": jax.random.randint(part_keys[1], (1,), 0, DATES).astype(jnp.int32),
    }


LOADING = 0.25

def window_counts(line_count, column_count, first_column, strip_columns, half_lines, half_columns):
    line_index = jnp.arange(line_count, dtype=jnp.int32)
    column_index = first_column + jnp.arange(column_count, dtype=jnp.int32)
    line_span = jnp.minimum(line_index + half_lines, line_count - 1) - jnp.maximum(line_index - half_lines, 0) + 1
    column_span = jnp.minimum(column_index + half_columns, strip_columns - 1) - jnp.maximum(column_index - half_columns, 0) + 1
    return line_span.astype(jnp.float32)[:, None] * column_span.astype(jnp.float32)[None, :]

def box_window(products, column_count, half_lines, half_columns):
    summed = products[..., 0:column_count]
    for offset in range(1, 2 * half_columns + 1):
        summed = summed + products[..., offset:offset + column_count]
    line_count = summed.shape[-2]
    widths = [(0, 0)] * (summed.ndim - 2) + [(half_lines, half_lines), (0, 0)]
    padded = jnp.pad(summed, widths)
    result = padded[..., 0:line_count, :]
    for offset in range(1, 2 * half_lines + 1):
        result = result + padded[..., offset:offset + line_count, :]
    return result

def tile_covariance(window_data, counts, column_count):
    real_part = window_data[0]
    imag_part = window_data[1]

    def one_date(date_index):
        real_one = lax.dynamic_index_in_dim(real_part, date_index, 0, keepdims=True)
        imag_one = lax.dynamic_index_in_dim(imag_part, date_index, 0, keepdims=True)
        product_real = real_one * real_part + imag_one * imag_part
        product_imag = imag_one * real_part - real_one * imag_part
        stacked = jnp.stack([product_real, product_imag])
        return (box_window(stacked, column_count, HALF_Y, HALF_X) / counts).astype(jnp.bfloat16)
    return lax.map(one_date, jnp.arange(real_part.shape[0], dtype=jnp.int32))

def dct_table(line_count):
    frequency = jnp.arange(line_count, dtype=jnp.float32)[:, None]
    position = jnp.arange(line_count, dtype=jnp.float32)[None, :]
    weight = jnp.where(frequency == 0, math.sqrt(1.0 / line_count), math.sqrt(2.0 / line_count))
    return weight * jnp.cos(jnp.pi * (2.0 * position + 1.0) * frequency / (2.0 * line_count))

def process_tile(window_bf16, first_column, strip_columns, reference_date):
    window_data = window_bf16.astype(jnp.float32)
    column_count = window_data.shape[3] - 2 * HALF_X
    line_count = window_data.shape[2]
    counts = window_counts(line_count, column_count, first_column, strip_columns, HALF_Y, HALF_X)
    covariance = tile_covariance(window_data, counts, column_count)
    date_count = covariance.shape[0]
    pick = (jnp.arange(date_count, dtype=jnp.int32) == reference_date).astype(jnp.float32)[:, None, None]
    start_real = jnp.broadcast_to(pick, (date_count, line_count, column_count))
    start_imag = jnp.zeros_like(start_real)

    def power_step(step_index, vector):
        vec_real, vec_imag = vector
        cov_real = covariance[:, 0].astype(jnp.float32)
        cov_imag = covariance[:, 1].astype(jnp.float32)
        new_real = lax.optimization_barrier(jnp.sum(cov_real * vec_real[None] - cov_imag * vec_imag[None], axis=1)) + LOADING * vec_real
        new_imag = lax.optimization_barrier(jnp.sum(cov_real * vec_imag[None] + cov_imag * vec_real[None], axis=1)) + LOADING * vec_imag
        length = jnp.sqrt(lax.optimization_barrier(jnp.sum(new_real * new_real + new_imag * new_imag, axis=0)))
        return (new_real / length, new_imag / length)
    vec_real, vec_imag = lax.fori_loop(0, POWER_ITERS, power_step, (start_real, start_imag))
    ref_real = lax.optimization_barrier(jnp.sum(vec_real * pick, axis=0))
    ref_imag = lax.optimization_barrier(jnp.sum(vec_imag * pick, axis=0))
    linked_real = DATES * (vec_real * ref_real + vec_imag * ref_imag)
    linked_imag = DATES * (vec_imag * ref_real - vec_real * ref_imag)
    center = window_data[..., HALF_X:HALF_X + column_count]
    scaling = 1.0 / math.sqrt(DATES)
    comp_real = lax.optimization_barrier(jnp.sum(linked_real * center[0] + linked_imag * center[1], axis=0)) * scaling
    comp_imag = lax.optimization_barrier(jnp.sum(linked_real * center[1] - linked_imag * center[0], axis=0)) * scaling
    linked_stack = jnp.stack([linked_real, linked_imag])
    table = dct_table(line_count)
    transformed = jnp.einsum('qr,pkrc->pkqc', table, linked_stack, precision=lax.Precision.HIGHEST)
    spectrum_tile = transformed.reshape(2, date_count * line_count, column_count)
    return (spectrum_tile, jnp.stack([comp_real, comp_imag]))

def reference(slcs, ref_date):
    stacked_data = slcs.reshape(2, DATES, ROWS, COLS)
    padded = jnp.pad(stacked_data, ((0, 0), (0, 0), (0, 0), (HALF_X, HALF_X)))

    def one_tile(tile_index):
        first_column = (tile_index * COLS_DEV).astype(jnp.int32)
        window_bf16 = lax.dynamic_slice_in_dim(padded, first_column, COLS_DEV + 2 * HALF_X, 3)
        return process_tile(window_bf16, first_column, COLS, ref_date[0])
    spectra, compressed_tiles = lax.map(one_tile, jnp.arange(N_PIX, dtype=jnp.int32))
    spectrum = jnp.transpose(spectra, (1, 2, 0, 3)).reshape(2, DATES * ROWS, COLS)
    compressed = jnp.transpose(compressed_tiles, (1, 2, 0, 3)).reshape(2, ROWS, COLS)
    return (spectrum, compressed)
```

```python
import functools
import math

import jax
import jax.numpy as jnp
from jax import lax
from jax.experimental import pallas as pl
from jax.experimental.pallas import tpu as pltpu
from jax.sharding import PartitionSpec as P

DATES = 16
ROWS = 64
HALF_X = 5
HALF_Y = 2
POWER_ITERS = 6
LOADING = 0.25

MARGIN = 8
PAIRS = DATES // 2
F32 = jnp.float32
BF16 = jnp.bfloat16


def iota(shape, dim):
    return lax.broadcasted_iota(jnp.int32, shape, dim)


def pack_kernel(x_ref, out_ref):
    devices = out_ref.shape[0]
    width = x_ref.shape[2] // devices
    zero = jnp.zeros((MARGIN, 2 * x_ref.shape[1]), BF16)
    out_ref[0, 0:MARGIN, :] = zero
    out_ref[devices - 1, width + MARGIN :, :] = zero
    for block in range(devices):
        columns = slice(block * width, (block + 1) * width)
        tile = jnp.concatenate([x_ref[0, :, columns], x_ref[1, :, columns]], axis=0)
        turned = tile.astype(F32).T.astype(BF16)
        out_ref[block, MARGIN : width + MARGIN, :] = turned
        if block > 0:
            out_ref[block - 1, width + MARGIN :, :] = turned[0:MARGIN]
        if block < devices - 1:
            out_ref[block + 1, 0:MARGIN, :] = turned[width - MARGIN :]


def split2(x):
    high = x.astype(BF16)
    return high, (x - high.astype(F32)).astype(BF16)


def inverse_counts(first_column, strip_columns, half):
    shape = (half, 2 * ROWS)
    lane = iota(shape, 1)
    line = lane % ROWS
    column = first_column + iota(shape, 0) + (lane // ROWS) * half
    lines = jnp.minimum(line + HALF_Y, ROWS - 1) - jnp.maximum(line - HALF_Y, 0) + 1
    columns = (
        jnp.minimum(column + HALF_X, strip_columns - 1) - jnp.maximum(column - HALF_X, 0) + 1
    )
    return 1.0 / (lines * columns).astype(F32)


def tree(terms):
    while len(terms) > 1:
        terms = [
            terms[k] + terms[k + 1] if k + 1 < len(terms) else terms[k]
            for k in range(0, len(terms), 2)
        ]
    return terms[0]


def entry(i, j):
    offset = (j - i) % DATES
    if offset <= PAIRS:
        return offset - 1, i, False
    return DATES - offset - 1, j, True


def link_kernel(
    strip_columns,
    scalar_ref,
    z_ref,
    linked_ref,
    comp_ref,
    window,
    center,
    prod,
    summed,
    cov_b,
    cov_f,
    diag,
    vec_b,
    vec_f,
    comp,
):
    half = center.shape[2]
    tall = window.shape[2]
    lanes = 2 * ROWS
    reference = scalar_ref[0]
    first_column = scalar_ref[1]

    low = iota((tall, lanes), 1) < ROWS

    def unmix(k, carry):
        top = z_ref[k, 0:tall, :].astype(F32)
        bottom = z_ref[k, half : half + tall, :].astype(F32)
        real = jnp.where(low, top, pltpu.roll(bottom, ROWS, 1))
        imag = jnp.where(low, pltpu.roll(top, ROWS, 1), bottom)
        window[k, 0] = real.astype(BF16)
        window[k, 1] = imag.astype(BF16)
        center[k, 0] = real[MARGIN : MARGIN + half]
        center[k, 1] = imag[MARGIN : MARGIN + half]
        return carry

    lax.fori_loop(0, DATES, unmix, 0)

    wide = 2 * lanes
    row, col = iota((wide, wide), 0), iota((wide, wide), 1)
    band_lines = jnp.where(
        (row // ROWS == col // ROWS) & (jnp.abs(row - col) <= HALF_Y), 1.0, 0.0
    ).astype(BF16)
    out_row, in_row = iota((half, tall), 0), iota((half, tall), 1)
    band_columns = jnp.where(jnp.abs(out_row + MARGIN - in_row) <= HALF_X, 1.0, 0.0).astype(BF16)
    inverse = inverse_counts(first_column, strip_columns, half)

    def pairs(i, carry):
        real, imag = window[i, 0], window[i, 1]
        for offset in range(1, PAIRS + 1):
            j = (i + offset) % DATES
            real_j, imag_j = window[j, 0], window[j, 1]
            at = slice((offset - 1) * tall, offset * tall)
            prod[at, 0:lanes] = real * real_j + imag * imag_j
            prod[at, lanes:] = imag * real_j - real * imag_j
        real32, imag32 = real.astype(F32), imag.astype(F32)
        high, rest = split2(real32 * real32 + imag32 * imag32)
        prod[PAIRS * tall :, 0:lanes] = high
        prod[PAIRS * tall :, lanes:] = rest
        sums = jnp.dot(prod[...], band_lines, preferred_element_type=F32)
        summed[0 : PAIRS * tall, :] = sums[0 : PAIRS * tall].astype(BF16)
        power = sums[PAIRS * tall :, 0:lanes] + sums[PAIRS * tall :, lanes:]
        high, rest = split2(power)
        summed[PAIRS * tall :, 0:lanes] = high
        summed[PAIRS * tall :, lanes:] = rest
        for offset in range(PAIRS + 1):
            at = slice(offset * tall, (offset + 1) * tall)
            box = jnp.dot(band_columns, summed[at, :], preferred_element_type=F32)
            if offset < PAIRS:
                for part in range(2):
                    value = box[:, part * lanes : (part + 1) * lanes] * inverse
                    cov_f[offset, i, part] = value
                    cov_b[offset, i, part] = value.astype(BF16)
            else:
                value = (box[:, 0:lanes] + box[:, lanes:]) * inverse
                diag[i] = value.astype(BF16).astype(F32) + LOADING
        return carry

    lax.fori_loop(0, DATES, pairs, 0)

    tile = 16

    def one_tile(g, carry):
        rows = pl.ds(pl.multiple_of(g * tile, tile), tile)

        for k in range(DATES):
            offset = (reference - k) % DATES
            plain = offset <= PAIRS
            slot = jnp.where(plain, jnp.maximum(offset, 1), DATES - offset) - 1
            date = jnp.where(plain, k, reference)
            sign = jnp.where(offset == 0, 0.0, jnp.where(plain, 1.0, -1.0)).astype(F32)
            real = cov_f[slot, date, 0, rows, :]
            real = jnp.where(offset == 0, diag[k, rows, :], real)
            imag = cov_f[slot, date, 1, rows, :] * sign
            vec_f[k, 0] = real
            vec_f[k, 1] = imag
            vec_b[k, 0] = real.astype(BF16)
            vec_b[k, 1] = imag.astype(BF16)

        def narrow_step(t, carry):
            real = [vec_b[k, 0] for k in range(DATES)]
            imag = [vec_b[k, 1] for k in range(DATES)]
            for i in range(DATES):
                terms_real, terms_imag = [], []
                for j in range(DATES):
                    if i == j:
                        continue
                    slot, date, conjugated = entry(i, j)
                    a = cov_b[slot, date, 0, rows, :]
                    b = cov_b[slot, date, 1, rows, :]
                    if conjugated:
                        terms_real.append(a * real[j] + b * imag[j])
                        terms_imag.append(a * imag[j] - b * real[j])
                    else:
                        terms_real.append(a * real[j] - b * imag[j])
                        terms_imag.append(a * imag[j] + b * real[j])
                own = diag[i, rows, :]
                new_real = own * vec_f[i, 0] + tree(terms_real).astype(F32)
                new_imag = own * vec_f[i, 1] + tree(terms_imag).astype(F32)
                vec_f[i, 0] = new_real
                vec_f[i, 1] = new_imag
                vec_b[i, 0] = new_real.astype(BF16)
                vec_b[i, 1] = new_imag.astype(BF16)
            return carry

        lax.fori_loop(0, POWER_ITERS - 2, narrow_step, 0)

        for sub in range(0, tile, 8):
            piece = slice(sub, sub + 8)
            at = pl.ds(pl.multiple_of(g * tile + sub, 8), 8)
            real = [vec_f[k, 0, piece] for k in range(DATES)]
            imag = [vec_f[k, 1, piece] for k in range(DATES)]
            squares = []
            for i in range(DATES):
                own = diag[i, at, :]
                new_real, new_imag = own * real[i], own * imag[i]
                for j in range(DATES):
                    if i == j:
                        continue
                    slot, date, conjugated = entry(i, j)
                    a = cov_f[slot, date, 0, at, :]
                    b = cov_f[slot, date, 1, at, :]
                    if conjugated:
                        new_real = new_real + (a * real[j] + b * imag[j])
                        new_imag = new_imag + (a * imag[j] - b * real[j])
                    else:
                        new_real = new_real + (a * real[j] - b * imag[j])
                        new_imag = new_imag + (a * imag[j] + b * real[j])
                vec_f[i, 0, piece] = new_real
                vec_f[i, 1, piece] = new_imag
                squares.append(new_real * new_real + new_imag * new_imag)
            scale = DATES / tree(squares)
            ref_real = vec_f[reference, 0, piece] * scale
            ref_imag = vec_f[reference, 1, piece] * scale
            comp_real = jnp.zeros((8, lanes), F32)
            comp_imag = jnp.zeros((8, lanes), F32)
            for k in range(DATES):
                real_k, imag_k = vec_f[k, 0, piece], vec_f[k, 1, piece]
                linked_real = real_k * ref_real + imag_k * ref_imag
                linked_imag = imag_k * ref_real - real_k * ref_imag
                z_real, z_imag = center[k, 0, at, :], center[k, 1, at, :]
                comp_real = comp_real + (linked_real * z_real + linked_imag * z_imag)
                comp_imag = comp_imag + (linked_real * z_imag - linked_imag * z_real)
                linked_ref[k, 0, at, :] = linked_real.astype(BF16)
                linked_ref[k, 1, at, :] = linked_imag.astype(BF16)
            comp[0, at, :] = comp_real * (1.0 / math.sqrt(DATES))
            comp[1, at, :] = comp_imag * (1.0 / math.sqrt(DATES))
        return carry

    lax.fori_loop(0, half // tile, one_tile, 0)

    for part in range(2):
        turned = comp[part].T
        comp_ref[part] = jnp.concatenate([turned[0:ROWS], turned[ROWS:]], axis=1)


def link(z, reference, first_column, strip_columns):
    width = z.shape[1] - 2 * MARGIN
    half = width // 2
    tall = half + 2 * MARGIN
    lanes = 2 * ROWS
    scalars = jnp.stack([reference, first_column])
    return pl.pallas_call(
        functools.partial(link_kernel, strip_columns),
        out_shape=(
            jax.ShapeDtypeStruct((DATES, 2, half, lanes), BF16),
            jax.ShapeDtypeStruct((2, ROWS, width), F32),
        ),
        in_specs=[
            pl.BlockSpec(memory_space=pltpu.SMEM),
            pl.BlockSpec(memory_space=pltpu.VMEM),
        ],
        out_specs=(
            pl.BlockSpec(memory_space=pltpu.VMEM),
            pl.BlockSpec(memory_space=pltpu.VMEM),
        ),
        scratch_shapes=[
            pltpu.VMEM((DATES, 2, tall, lanes), BF16),
            pltpu.VMEM((DATES, 2, half, lanes), F32),
            pltpu.VMEM(((PAIRS + 1) * tall, 2 * lanes), BF16),
            pltpu.VMEM(((PAIRS + 1) * tall, 2 * lanes), BF16),
            pltpu.VMEM((PAIRS, DATES, 2, half, lanes), BF16),
            pltpu.VMEM((PAIRS, DATES, 2, half, lanes), F32),
            pltpu.VMEM((DATES, half, lanes), F32),
            pltpu.VMEM((DATES, 2, 16, lanes), BF16),
            pltpu.VMEM((DATES, 2, 16, lanes), F32),
            pltpu.VMEM((2, half, lanes), F32),
        ],
        name="link",
    )(scalars, z)


def dct_table(line_count):
    frequency = jnp.arange(line_count, dtype=F32)[:, None]
    position = jnp.arange(line_count, dtype=F32)[None, :]
    weight = jnp.where(frequency == 0, math.sqrt(1.0 / line_count), math.sqrt(2.0 / line_count))
    return weight * jnp.cos(jnp.pi * (2.0 * position + 1.0) * frequency / (2.0 * line_count))


def dct_kernel(table_ref, x_ref, out_ref):
    sources, parts, half, lanes = x_ref.shape
    low = iota((half, lanes), 1) < ROWS
    table = jnp.concatenate([table_ref[...], table_ref[...]], axis=1)
    high, rest = split2(table)
    left = jnp.concatenate([high, rest], axis=1)
    for source in range(sources):
        for part in range(parts):
            x = x_ref[source, part].astype(F32)
            both = jnp.concatenate(
                [jnp.where(low, x, 0.0), jnp.where(low, 0.0, x)], axis=0
            ).astype(BF16)
            right = jnp.concatenate([both, both], axis=1)
            out_ref[part, :, source * 2 * half : (source + 1) * 2 * half] = lax.dot_general(
                left, right, (((1,), (1,)), ((), ())), preferred_element_type=F32
            )


def transform(linked):
    sources, parts, half, _ = linked.shape
    return pl.pallas_call(
        dct_kernel,
        out_shape=jax.ShapeDtypeStruct((parts, ROWS, sources * 2 * half), F32),
        in_specs=[pl.BlockSpec(memory_space=pltpu.VMEM)] * 2,
        out_specs=pl.BlockSpec(memory_space=pltpu.VMEM),
        name="transform",
    )(dct_table(ROWS), linked)


def exchange(blocks):
    return lax.all_to_all(blocks, "pix", split_axis=0, concat_axis=0, tiled=True)


def whole_dates(slcs, reference, first_column, strip_columns):
    devices = lax.axis_size("pix")
    width = strip_columns // devices
    packed = pl.pallas_call(
        pack_kernel,
        out_shape=jax.ShapeDtypeStruct((devices, width + 2 * MARGIN, 2 * ROWS), BF16),
        in_specs=[pl.BlockSpec(memory_space=pltpu.VMEM)],
        out_specs=pl.BlockSpec(memory_space=pltpu.VMEM),
        name="pack",
    )(slcs)
    linked, compressed = link(exchange(packed), reference, first_column, strip_columns)
    return transform(exchange(linked)), compressed


def parts_of_dates(slcs, reference, first_column, strip_columns):
    devices = lax.axis_size("pix")
    width = strip_columns // devices
    local_rows = slcs.shape[1]
    padded = jnp.pad(slcs, ((0, 0), (0, 0), (MARGIN, MARGIN)))
    blocks = jnp.stack(
        [padded[:, :, d * width : d * width + width + 2 * MARGIN] for d in range(devices)]
    )
    window = exchange(blocks)
    per_date = ROWS // local_rows
    window = window.reshape(DATES, per_date, 2, local_rows, width + 2 * MARGIN)
    z = window.transpose(0, 4, 2, 1, 3).reshape(DATES, width + 2 * MARGIN, 2 * ROWS)
    linked, compressed = link(z, reference, first_column, strip_columns)
    linked = linked.astype(F32).reshape(DATES, 2, width // 2, 2, ROWS)
    spectrum = jnp.einsum(
        "qr,kpchr->kqphc", dct_table(ROWS), linked, precision=lax.Precision.HIGHEST
    ).reshape(DATES * ROWS // local_rows, local_rows, 2, width)
    arrived = exchange(spectrum.astype(BF16))
    spectrum = arrived.transpose(2, 1, 0, 3).reshape(2, local_rows, strip_columns)
    return spectrum.astype(F32), compressed


def on_device(slcs, ref_date):
    devices = lax.axis_size("pix")
    strip_columns = slcs.shape[2]
    first_column = lax.axis_index("pix") * (strip_columns // devices)
    plan = whole_dates if slcs.shape[1] == ROWS else parts_of_dates
    return plan(slcs, ref_date[0], first_column, strip_columns)


def solution(mesh):
    return jax.shard_map(
        on_device,
        mesh=mesh,
        in_specs=(P(None, ("grp", "pix"), None), P("grp")),
        out_specs=(P(None, ("grp", "pix"), None), P(None, None, ("grp", "pix"))),
        check_vma=False,
    )
```

```python
import functools
import math

import jax
import jax.numpy as jnp
from jax import lax
from jax.experimental import pallas as pl
from jax.experimental.pallas import tpu as pltpu
from jax.sharding import PartitionSpec as P

DATES = 16
ROWS = 64
HALF_X = 5
HALF_Y = 2
POWER_ITERS = 6
LOADING = 0.25

MARGIN = 8
TILE = 16
GROUP = 4
PAIRS = DATES // 2
F32 = jnp.float32
BF16 = jnp.bfloat16


def iota(shape, dim):
    return lax.broadcasted_iota(jnp.int32, shape, dim)


def pack_kernel(x_ref, out_ref):
    devices = out_ref.shape[0]
    width = x_ref.shape[2] // devices
    zero = jnp.zeros((MARGIN, 2 * x_ref.shape[1]), BF16)
    out_ref[0, 0:MARGIN, :] = zero
    out_ref[devices - 1, width + MARGIN :, :] = zero
    for block in range(devices):
        columns = slice(block * width, (block + 1) * width)
        tile = jnp.concatenate([x_ref[0, :, columns], x_ref[1, :, columns]], axis=0)
        turned = tile.astype(F32).T.astype(BF16)
        out_ref[block, MARGIN : width + MARGIN, :] = turned
        if block > 0:
            out_ref[block - 1, width + MARGIN :, :] = turned[0:MARGIN]
        if block < devices - 1:
            out_ref[block + 1, 0:MARGIN, :] = turned[width - MARGIN :]


def split2(x):
    high = x.astype(BF16)
    return high, (x - high.astype(F32)).astype(BF16)


def inverse_counts(first_column, strip_columns, half):
    shape = (half, 2 * ROWS)
    lane = iota(shape, 1)
    line = lane % ROWS
    column = first_column + iota(shape, 0) + (lane // ROWS) * half
    lines = jnp.minimum(line + HALF_Y, ROWS - 1) - jnp.maximum(line - HALF_Y, 0) + 1
    columns = (
        jnp.minimum(column + HALF_X, strip_columns - 1) - jnp.maximum(column - HALF_X, 0) + 1
    )
    return 1.0 / (lines * columns).astype(F32)


def tree(terms):
    while len(terms) > 1:
        terms = [
            terms[k] + terms[k + 1] if k + 1 < len(terms) else terms[k]
            for k in range(0, len(terms), 2)
        ]
    return terms[0]


def entry(i, j):
    offset = (j - i) % DATES
    if offset <= PAIRS:
        return offset - 1, i, False
    return DATES - offset - 1, j, True


def packed(x):
    return x.astype(F32).astype(BF16)


def link_kernel(
    strip_columns,
    scalar_ref,
    z_ref,
    linked_ref,
    comp_ref,
    window,
    center,
    summed_even,
    summed_odd,
    cov,
    diag,
    vec,
    narrow,
    comp,
):
    half = center.shape[2]
    tall = window.shape[2]
    lanes = 2 * ROWS
    reference = scalar_ref[0]
    first_column = scalar_ref[1]

    low = iota((tall, lanes), 1) < ROWS

    def unmix(k, carry):
        top = z_ref[k, 0:tall, :].astype(F32)
        bottom = z_ref[k, half : half + tall, :].astype(F32)
        real = jnp.where(low, top, pltpu.roll(bottom, ROWS, 1))
        imag = jnp.where(low, pltpu.roll(top, ROWS, 1), bottom)
        window[k, 0] = real.astype(BF16)
        window[k, 1] = imag.astype(BF16)
        center[k, 0] = real[MARGIN : MARGIN + half]
        center[k, 1] = imag[MARGIN : MARGIN + half]
        return carry

    lax.fori_loop(0, DATES, unmix, 0)

    wide = 2 * lanes
    row, col = iota((wide, wide), 0), iota((wide, wide), 1)
    band_lines = jnp.where(
        (row // ROWS == col // ROWS) & (jnp.abs(row - col) <= HALF_Y), 1.0, 0.0
    ).astype(BF16)
    out_row, in_row = iota((half, tall), 0), iota((half, tall), 1)
    band_columns = jnp.where(jnp.abs(out_row + MARGIN - in_row) <= HALF_X, 1.0, 0.0).astype(BF16)
    inverse = inverse_counts(first_column, strip_columns, half)

    def sum_lines(i, summed):
        real, imag = packed(window[i, 0]), packed(window[i, 1])
        left, right = [], []
        for offset in range(1, PAIRS + 1):
            j = (i + offset) % DATES
            real_j, imag_j = packed(window[j, 0]), packed(window[j, 1])
            left.append(real * real_j + imag * imag_j)
            right.append(imag * real_j - real * imag_j)
        real32, imag32 = real.astype(F32), imag.astype(F32)
        high, rest = split2(real32 * real32 + imag32 * imag32)
        left.append(high)
        right.append(rest)
        products = jnp.concatenate(
            [jnp.concatenate(left, axis=0), jnp.concatenate(right, axis=0)], axis=1
        )
        sums = jnp.dot(products, band_lines, preferred_element_type=F32)
        summed[0, 0 : PAIRS * tall] = sums[0 : PAIRS * tall, 0:lanes].astype(BF16)
        summed[1, 0 : PAIRS * tall] = sums[0 : PAIRS * tall, lanes:].astype(BF16)
        power = sums[PAIRS * tall :, 0:lanes] + sums[PAIRS * tall :, lanes:]
        high, rest = split2(power)
        summed[0, PAIRS * tall :] = high
        summed[1, PAIRS * tall :] = rest

    def sum_columns(i, summed):
        for offset in range(PAIRS + 1):
            at = slice(offset * tall, (offset + 1) * tall)
            right = jnp.concatenate([packed(summed[0, at]), packed(summed[1, at])], axis=1)
            box = jnp.dot(band_columns, right, preferred_element_type=F32)
            if offset < PAIRS:
                for part in range(2):
                    value = (box[:, part * lanes : (part + 1) * lanes] * inverse).astype(BF16)
                    for g in range(half // TILE):
                        cov[g, offset, i, part] = value[g * TILE : (g + 1) * TILE]
            else:
                value = (box[:, 0:lanes] + box[:, lanes:]) * inverse
                value = value.astype(BF16).astype(F32) + LOADING
                for g in range(half // TILE):
                    diag[g, i] = value[g * TILE : (g + 1) * TILE]

    sum_lines(0, summed_even)

    def two_dates(n, carry):
        sum_lines(2 * n + 1, summed_odd)
        sum_columns(2 * n, summed_even)
        sum_lines(jnp.minimum(2 * n + 2, DATES - 1), summed_even)
        sum_columns(2 * n + 1, summed_odd)
        return carry

    lax.fori_loop(0, DATES // 2, two_dates, 0)

    def first_step(k, carry):
        offset = (reference + DATES - k) % DATES
        plain = offset <= PAIRS
        slot = jnp.where(plain, jnp.maximum(offset, 1), DATES - offset) - 1
        date = jnp.where(plain, k, reference)
        sign = jnp.where(offset == 0, 0.0, jnp.where(plain, 1.0, -1.0)).astype(F32)
        for g in range(half // TILE):
            real = jnp.where(offset == 0, diag[g, k], cov[g, slot, date, 0].astype(F32))
            imag = cov[g, slot, date, 1].astype(F32) * sign
            vec[g, k, 0] = real
            vec[g, k, 1] = imag
            narrow[g, k, 0] = real.astype(BF16)
            narrow[g, k, 1] = imag.astype(BF16)
        return carry

    lax.fori_loop(0, DATES, first_step, 0)

    def one_tile(g, carry):
        def step(last):
            real = [packed(narrow[g, k, 0]) for k in range(DATES)]
            imag = [packed(narrow[g, k, 1]) for k in range(DATES)]
            for i in range(DATES):
                own = diag[g, i]
                total = [own * vec[g, i, 0], own * vec[g, i, 1]]
                sums = [None, None]
                others = [j for j in range(DATES) if j != i]
                for at in range(0, len(others), GROUP):
                    terms = [], []
                    for j in others[at : at + GROUP]:
                        slot, date, conjugated = entry(i, j)
                        a = packed(cov[g, slot, date, 0])
                        b = packed(cov[g, slot, date, 1])
                        if conjugated:
                            terms[0].append(a * real[j] + b * imag[j])
                            terms[1].append(a * imag[j] - b * real[j])
                        else:
                            terms[0].append(a * real[j] - b * imag[j])
                            terms[1].append(a * imag[j] + b * real[j])
                    for part in range(2):
                        term = tree(terms[part])
                        if last:
                            total[part] = total[part] + term.astype(F32)
                        else:
                            sums[part] = term if at == 0 else sums[part] + term
                for part in range(2):
                    if not last:
                        total[part] = total[part] + sums[part].astype(F32)
                        narrow[g, i, part] = total[part].astype(BF16)
                    vec[g, i, part] = total[part]

        def early_step(t, carry):
            step(False)
            return carry

        lax.fori_loop(0, POWER_ITERS - 2, early_step, 0)
        step(True)

        for sub in range(0, TILE, 8):
            at = slice(sub, sub + 8)
            rows = pl.ds(pl.multiple_of(g * TILE + sub, 8), 8)
            squares = []
            for k in range(DATES):
                real, imag = vec[g, k, 0, at], vec[g, k, 1, at]
                squares.append(real * real + imag * imag)
            scale = DATES / tree(squares)
            ref_real = vec[g, reference, 0, at] * scale
            ref_imag = vec[g, reference, 1, at] * scale
            comp_real = comp_imag = None
            for k in range(DATES):
                real, imag = vec[g, k, 0, at], vec[g, k, 1, at]
                linked_real = real * ref_real + imag * ref_imag
                linked_imag = imag * ref_real - real * ref_imag
                z_real, z_imag = center[k, 0, rows, :], center[k, 1, rows, :]
                more_real = linked_real * z_real + linked_imag * z_imag
                more_imag = linked_real * z_imag - linked_imag * z_real
                comp_real = more_real if k == 0 else comp_real + more_real
                comp_imag = more_imag if k == 0 else comp_imag + more_imag
                linked_ref[k, 0, rows, :] = linked_real.astype(BF16)
                linked_ref[k, 1, rows, :] = linked_imag.astype(BF16)
            comp[0, rows, :] = comp_real * (1.0 / math.sqrt(DATES))
            comp[1, rows, :] = comp_imag * (1.0 / math.sqrt(DATES))
        return carry

    lax.fori_loop(0, half // TILE, one_tile, 0)

    for part in range(2):
        turned = comp[part].T
        comp_ref[part] = jnp.concatenate([turned[0:ROWS], turned[ROWS:]], axis=1)


def link(z, reference, first_column, strip_columns):
    width = z.shape[1] - 2 * MARGIN
    half = width // 2
    tall = half + 2 * MARGIN
    lanes = 2 * ROWS
    scalars = jnp.stack([reference, first_column])
    return pl.pallas_call(
        functools.partial(link_kernel, strip_columns),
        out_shape=(
            jax.ShapeDtypeStruct((DATES, 2, half, lanes), BF16),
            jax.ShapeDtypeStruct((2, ROWS, width), F32),
        ),
        in_specs=[
            pl.BlockSpec(memory_space=pltpu.SMEM),
            pl.BlockSpec(memory_space=pltpu.VMEM),
        ],
        out_specs=(
            pl.BlockSpec(memory_space=pltpu.VMEM),
            pl.BlockSpec(memory_space=pltpu.VMEM),
        ),
        scratch_shapes=[
            pltpu.VMEM((DATES, 2, tall, lanes), BF16),
            pltpu.VMEM((DATES, 2, half, lanes), F32),
            pltpu.VMEM((2, (PAIRS + 1) * tall, lanes), BF16),
            pltpu.VMEM((2, (PAIRS + 1) * tall, lanes), BF16),
            pltpu.VMEM((half // TILE, PAIRS, DATES, 2, TILE, lanes), BF16),
            pltpu.VMEM((half // TILE, DATES, TILE, lanes), F32),
            pltpu.VMEM((half // TILE, DATES, 2, TILE, lanes), F32),
            pltpu.VMEM((half // TILE, DATES, 2, TILE, lanes), BF16),
            pltpu.VMEM((2, half, lanes), F32),
        ],
        name="link",
    )(scalars, z)


def dct_table(line_count):
    frequency = jnp.arange(line_count, dtype=F32)[:, None]
    position = jnp.arange(line_count, dtype=F32)[None, :]
    weight = jnp.where(frequency == 0, math.sqrt(1.0 / line_count), math.sqrt(2.0 / line_count))
    return weight * jnp.cos(jnp.pi * (2.0 * position + 1.0) * frequency / (2.0 * line_count))


def dct_kernel(table_ref, x_ref, out_ref):
    sources, parts, half, lanes = x_ref.shape
    low = iota((half, lanes), 1) < ROWS
    table = jnp.concatenate([table_ref[...], table_ref[...]], axis=1)
    high, rest = split2(table)
    left = jnp.concatenate([high, rest], axis=1)
    for source in range(sources):
        for part in range(parts):
            x = x_ref[source, part].astype(F32)
            both = jnp.concatenate(
                [jnp.where(low, x, 0.0), jnp.where(low, 0.0, x)], axis=0
            ).astype(BF16)
            right = jnp.concatenate([both, both], axis=1)
            out_ref[part, :, source * 2 * half : (source + 1) * 2 * half] = lax.dot_general(
                left, right, (((1,), (1,)), ((), ())), preferred_element_type=F32
            )


def transform(linked):
    sources, parts, half, _ = linked.shape
    return pl.pallas_call(
        dct_kernel,
        out_shape=jax.ShapeDtypeStruct((parts, ROWS, sources * 2 * half), F32),
        in_specs=[pl.BlockSpec(memory_space=pltpu.VMEM)] * 2,
        out_specs=pl.BlockSpec(memory_space=pltpu.VMEM),
        name="transform",
    )(dct_table(ROWS), linked)


def exchange(blocks):
    return lax.all_to_all(blocks, "pix", split_axis=0, concat_axis=0, tiled=True)


def whole_dates(slcs, reference, first_column, strip_columns):
    devices = lax.axis_size("pix")
    width = strip_columns // devices
    packed = pl.pallas_call(
        pack_kernel,
        out_shape=jax.ShapeDtypeStruct((devices, width + 2 * MARGIN, 2 * ROWS), BF16),
        in_specs=[pl.BlockSpec(memory_space=pltpu.VMEM)],
        out_specs=pl.BlockSpec(memory_space=pltpu.VMEM),
        name="pack",
    )(slcs)
    linked, compressed = link(exchange(packed), reference, first_column, strip_columns)
    return transform(exchange(linked)), compressed


def parts_of_dates(slcs, reference, first_column, strip_columns):
    devices = lax.axis_size("pix")
    width = strip_columns // devices
    local_rows = slcs.shape[1]
    padded = jnp.pad(slcs, ((0, 0), (0, 0), (MARGIN, MARGIN)))
    blocks = jnp.stack(
        [padded[:, :, d * width : d * width + width + 2 * MARGIN] for d in range(devices)]
    )
    window = exchange(blocks)
    per_date = ROWS // local_rows
    window = window.reshape(DATES, per_date, 2, local_rows, width + 2 * MARGIN)
    z = window.transpose(0, 4, 2, 1, 3).reshape(DATES, width + 2 * MARGIN, 2 * ROWS)
    linked, compressed = link(z, reference, first_column, strip_columns)
    linked = linked.astype(F32).reshape(DATES, 2, width // 2, 2, ROWS)
    spectrum = jnp.einsum(
        "qr,kpchr->kqphc", dct_table(ROWS), linked, precision=lax.Precision.HIGHEST
    ).reshape(DATES * ROWS // local_rows, local_rows, 2, width)
    arrived = exchange(spectrum.astype(BF16))
    spectrum = arrived.transpose(2, 1, 0, 3).reshape(2, local_rows, strip_columns)
    return spectrum.astype(F32), compressed


def on_device(slcs, ref_date):
    devices = lax.axis_size("pix")
    strip_columns = slcs.shape[2]
    first_column = lax.axis_index("pix") * (strip_columns // devices)
    plan = whole_dates if slcs.shape[1] == ROWS else parts_of_dates
    return plan(slcs, ref_date[0], first_column, strip_columns)


def solution(mesh):
    return jax.shard_map(
        on_device,
        mesh=mesh,
        in_specs=(P(None, ("grp", "pix"), None), P("grp")),
        out_specs=(P(None, ("grp", "pix"), None), P(None, None, ("grp", "pix"))),
        check_vma=False,
    )
```

```python
import functools
import math

import jax
import jax.numpy as jnp
from jax import lax
from jax.experimental import pallas as pl
from jax.experimental.pallas import tpu as pltpu
from jax.sharding import PartitionSpec as P

DATES = 16
ROWS = 64
HALF_X = 5
HALF_Y = 2
POWER_ITERS = 6
LOADING = 0.25

CHUNKS = 1
MARGIN = 8
TILE = 16
UNROLL = 4
GROUP = 4
PAIRS = DATES // 2
F32 = jnp.float32
BF16 = jnp.bfloat16
OUT = pltpu.VMEM


def iota(shape, dim):
    return lax.broadcasted_iota(jnp.int32, shape, dim)


def in_vmem(*arrays):
    return [pltpu.with_memory_space_constraint(x, pltpu.VMEM) for x in arrays]


def pack_kernel(chunk, chunks, x_ref, out_ref):
    devices, tall, _ = out_ref.shape
    width = (tall - 2 * MARGIN) * chunks
    first = chunk * (tall - 2 * MARGIN) - MARGIN
    zero = jnp.zeros((MARGIN, 2 * x_ref.shape[1]), BF16)
    if chunk == 0:
        out_ref[0, 0:MARGIN, :] = zero
    if chunk == chunks - 1:
        out_ref[devices - 1, tall - MARGIN :, :] = zero
    for block in range(devices):
        columns = slice(block * width, (block + 1) * width)
        tile = jnp.concatenate([x_ref[0, :, columns], x_ref[1, :, columns]], axis=0)
        turned = tile.astype(F32).T.astype(BF16)
        low, high = max(first, 0), min(first + tall, width)
        out_ref[block, low - first : high - first, :] = turned[low:high]
        if chunk == chunks - 1 and block > 0:
            out_ref[block - 1, tall - MARGIN :, :] = turned[0:MARGIN]
        if chunk == 0 and block < devices - 1:
            out_ref[block + 1, 0:MARGIN, :] = turned[width - MARGIN :]


def pack(slcs, chunk, chunks, devices):
    _, lines, columns = slcs.shape
    tall = columns // devices // chunks + 2 * MARGIN
    return pl.pallas_call(
        functools.partial(pack_kernel, chunk, chunks),
        out_shape=OUT((devices, tall, 2 * lines), BF16),
        in_specs=[pl.BlockSpec(memory_space=pltpu.VMEM)],
        out_specs=pl.BlockSpec(memory_space=pltpu.VMEM),
        cost_estimate=pl.CostEstimate(
            flops=4 * lines * columns, bytes_accessed=8 * lines * columns, transcendentals=0
        ),
        name="pack",
    )(*in_vmem(slcs))


def split2(x):
    high = x.astype(BF16)
    return high, (x - high.astype(F32)).astype(BF16)


def inverse_counts(first_column, strip_columns, half):
    shape = (half, 2 * ROWS)
    lane = iota(shape, 1)
    line = lane % ROWS
    column = first_column + iota(shape, 0) + (lane // ROWS) * half
    lines = jnp.minimum(line + HALF_Y, ROWS - 1) - jnp.maximum(line - HALF_Y, 0) + 1
    columns = (
        jnp.minimum(column + HALF_X, strip_columns - 1) - jnp.maximum(column - HALF_X, 0) + 1
    )
    return 1.0 / (lines * columns).astype(F32)


def tree(terms):
    while len(terms) > 1:
        terms = [
            terms[k] + terms[k + 1] if k + 1 < len(terms) else terms[k]
            for k in range(0, len(terms), 2)
        ]
    return terms[0]


def entry(i, j):
    offset = (j - i) % DATES
    if offset <= PAIRS:
        return offset - 1, i, False
    return DATES - offset - 1, j, True


def packed(x):
    return x.astype(F32).astype(BF16)


def link_kernel(
    strip_columns,
    offset,
    reference_ref,
    z_ref,
    linked_ref,
    comp_ref,
    window,
    center,
    summed_even,
    summed_odd,
    cov,
    diag,
    vec,
    narrow,
    comp,
):
    half = center.shape[2]
    tall = window.shape[2]
    lanes = 2 * ROWS
    reference = reference_ref[0]
    first_column = lax.axis_index("pix") * (strip_columns // lax.axis_size("pix")) + offset

    low = iota((tall, lanes), 1) < ROWS

    def unmix(n, carry):
        for u in range(UNROLL):
            k = n * UNROLL + u
            top = z_ref[k, 0:tall, :].astype(F32)
            bottom = z_ref[k, half : half + tall, :].astype(F32)
            real = jnp.where(low, top, pltpu.roll(bottom, ROWS, 1))
            imag = jnp.where(low, pltpu.roll(top, ROWS, 1), bottom)
            window[k, 0] = real.astype(BF16)
            window[k, 1] = imag.astype(BF16)
            center[k, 0] = real[MARGIN : MARGIN + half]
            center[k, 1] = imag[MARGIN : MARGIN + half]
        return carry

    lax.fori_loop(0, DATES // UNROLL, unmix, 0)

    wide = 2 * lanes
    row, col = iota((wide, wide), 0), iota((wide, wide), 1)
    band_lines = jnp.where(
        (row // ROWS == col // ROWS) & (jnp.abs(row - col) <= HALF_Y), 1.0, 0.0
    ).astype(BF16)
    out_row, in_row = iota((half, tall), 0), iota((half, tall), 1)
    band_columns = jnp.where(jnp.abs(out_row + MARGIN - in_row) <= HALF_X, 1.0, 0.0).astype(BF16)
    inverse = inverse_counts(first_column, strip_columns, half)

    def sum_columns(i, slot, summed):
        real, imag = packed(window[i, 0]), packed(window[i, 1])
        real32, imag32 = real.astype(F32), imag.astype(F32)
        for offset in range(1, PAIRS + 2):
            if offset <= PAIRS:
                j = (i + offset) % DATES
                real_j, imag_j = packed(window[j, 0]), packed(window[j, 1])
                left = real * real_j + imag * imag_j
                right = imag * real_j - real * imag_j
            else:
                left, right = split2(real32 * real32 + imag32 * imag32)
            sums = jnp.dot(
                band_columns,
                jnp.concatenate([left, right], axis=1),
                preferred_element_type=F32,
            )
            left, right = sums[:, 0:lanes], sums[:, lanes:]
            if offset <= PAIRS:
                left, right = left.astype(BF16), right.astype(BF16)
            else:
                left, right = split2(left + right)
            at = (slot * (PAIRS + 1) + offset - 1) * half
            summed[0, at : at + half] = left
            summed[1, at : at + half] = right

    def sum_lines(i, summed):
        both = jnp.concatenate([packed(summed[0]), packed(summed[1])], axis=1)
        boxes = jnp.dot(both, band_lines, preferred_element_type=F32)
        for slot in range(2):
            for offset in range(PAIRS + 1):
                at = (slot * (PAIRS + 1) + offset) * half
                box = boxes[at : at + half]
                if offset < PAIRS:
                    for part in range(2):
                        value = box[:, part * lanes : (part + 1) * lanes] * inverse
                        value = value.astype(BF16)
                        for g in range(half // TILE):
                            cov[g, offset, i + slot, part] = value[g * TILE : (g + 1) * TILE]
                else:
                    value = (box[:, 0:lanes] + box[:, lanes:]) * inverse
                    value = value.astype(BF16).astype(F32) + LOADING
                    for g in range(half // TILE):
                        diag[g, i + slot] = value[g * TILE : (g + 1) * TILE]

    def columns_of_two(i, summed):
        for slot in range(2):
            sum_columns(i + slot, slot, summed)

    columns_of_two(0, summed_even)

    def four_dates(n, carry):
        columns_of_two(4 * n + 2, summed_odd)
        sum_lines(4 * n, summed_even)
        columns_of_two(jnp.minimum(4 * n + 4, DATES - 2), summed_even)
        sum_lines(4 * n + 2, summed_odd)
        return carry

    lax.fori_loop(0, DATES // 4, four_dates, 0)

    def first_step(k, carry):
        offset = (reference + DATES - k) % DATES
        plain = offset <= PAIRS
        slot = jnp.where(plain, jnp.maximum(offset, 1), DATES - offset) - 1
        date = jnp.where(plain, k, reference)
        sign = jnp.where(offset == 0, 0.0, jnp.where(plain, 1.0, -1.0)).astype(F32)
        for g in range(half // TILE):
            real = jnp.where(offset == 0, diag[g, k], cov[g, slot, date, 0].astype(F32))
            imag = cov[g, slot, date, 1].astype(F32) * sign
            vec[g, k, 0] = real
            vec[g, k, 1] = imag
            narrow[g, k, 0] = real.astype(BF16)
            narrow[g, k, 1] = imag.astype(BF16)
        return carry

    lax.fori_loop(0, DATES, first_step, 0)

    def one_tile(g, carry):
        def step(last):
            real = [packed(narrow[g, k, 0]) for k in range(DATES)]
            imag = [packed(narrow[g, k, 1]) for k in range(DATES)]
            for i in range(DATES):
                own = diag[g, i]
                total = [own * vec[g, i, 0], own * vec[g, i, 1]]
                sums = [None, None]
                others = [j for j in range(DATES) if j != i]
                for at in range(0, len(others), GROUP):
                    terms = [], []
                    for j in others[at : at + GROUP]:
                        slot, date, conjugated = entry(i, j)
                        a = packed(cov[g, slot, date, 0])
                        b = packed(cov[g, slot, date, 1])
                        if conjugated:
                            terms[0].append(a * real[j] + b * imag[j])
                            terms[1].append(a * imag[j] - b * real[j])
                        else:
                            terms[0].append(a * real[j] - b * imag[j])
                            terms[1].append(a * imag[j] + b * real[j])
                    for part in range(2):
                        term = tree(terms[part])
                        if last:
                            total[part] = total[part] + term.astype(F32)
                        else:
                            sums[part] = term if at == 0 else sums[part] + term
                for part in range(2):
                    if not last:
                        total[part] = total[part] + sums[part].astype(F32)
                        narrow[g, i, part] = total[part].astype(BF16)
                    vec[g, i, part] = total[part]

        def early_step(t, carry):
            step(False)
            return carry

        lax.fori_loop(0, POWER_ITERS - 2, early_step, 0)
        step(True)

        for sub in range(0, TILE, 8):
            at = slice(sub, sub + 8)
            rows = pl.ds(pl.multiple_of(g * TILE + sub, 8), 8)
            squares = []
            for k in range(DATES):
                real, imag = vec[g, k, 0, at], vec[g, k, 1, at]
                squares.append(real * real + imag * imag)
            scale = DATES / tree(squares)
            ref_real = vec[g, reference, 0, at] * scale
            ref_imag = vec[g, reference, 1, at] * scale
            comp_real = comp_imag = None
            for k in range(DATES):
                real, imag = vec[g, k, 0, at], vec[g, k, 1, at]
                linked_real = real * ref_real + imag * ref_imag
                linked_imag = imag * ref_real - real * ref_imag
                z_real, z_imag = center[k, 0, rows, :], center[k, 1, rows, :]
                more_real = linked_real * z_real + linked_imag * z_imag
                more_imag = linked_real * z_imag - linked_imag * z_real
                comp_real = more_real if k == 0 else comp_real + more_real
                comp_imag = more_imag if k == 0 else comp_imag + more_imag
                linked_ref[k, 0, rows, :] = linked_real.astype(BF16)
                linked_ref[k, 1, rows, :] = linked_imag.astype(BF16)
            comp[0, rows, :] = comp_real * (1.0 / math.sqrt(DATES))
            comp[1, rows, :] = comp_imag * (1.0 / math.sqrt(DATES))
        return carry

    lax.fori_loop(0, half // TILE, one_tile, 0)

    for part in range(2):
        turned = comp[part].T
        comp_ref[part] = jnp.concatenate([turned[0:ROWS], turned[ROWS:]], axis=1)


def link(z, reference, offset, strip_columns):
    width = z.shape[1] - 2 * MARGIN
    half = width // 2
    tall = half + 2 * MARGIN
    lanes = 2 * ROWS
    return pl.pallas_call(
        functools.partial(link_kernel, strip_columns, offset),
        out_shape=(
            OUT((DATES, 2, half, lanes), BF16),
            OUT((2, ROWS, width), F32),
        ),
        in_specs=[
            pl.BlockSpec(memory_space=pltpu.SMEM),
            pl.BlockSpec(memory_space=pltpu.VMEM),
        ],
        out_specs=(
            pl.BlockSpec(memory_space=pltpu.VMEM),
            pl.BlockSpec(memory_space=pltpu.VMEM),
        ),
        scratch_shapes=[
            pltpu.VMEM((DATES, 2, tall, lanes), BF16),
            pltpu.VMEM((DATES, 2, half, lanes), F32),
            pltpu.VMEM((2, 2 * (PAIRS + 1) * half, lanes), BF16),
            pltpu.VMEM((2, 2 * (PAIRS + 1) * half, lanes), BF16),
            pltpu.VMEM((half // TILE, PAIRS, DATES, 2, TILE, lanes), BF16),
            pltpu.VMEM((half // TILE, DATES, TILE, lanes), F32),
            pltpu.VMEM((half // TILE, DATES, 2, TILE, lanes), F32),
            pltpu.VMEM((half // TILE, DATES, 2, TILE, lanes), BF16),
            pltpu.VMEM((2, half, lanes), F32),
        ],
        cost_estimate=pl.CostEstimate(
            flops=16 * DATES * DATES * POWER_ITERS * width * ROWS,
            bytes_accessed=6 * DATES * width * ROWS,
            transcendentals=0,
        ),
        name="link",
    )(reference, *in_vmem(z))


def dct_table(line_count):
    frequency = jnp.arange(line_count, dtype=F32)[:, None]
    position = jnp.arange(line_count, dtype=F32)[None, :]
    weight = jnp.where(frequency == 0, math.sqrt(1.0 / line_count), math.sqrt(2.0 / line_count))
    return weight * jnp.cos(jnp.pi * (2.0 * position + 1.0) * frequency / (2.0 * line_count))


def dct_kernel(table_ref, *refs):
    x_refs, out_ref = refs[:-1], refs[-1]
    sources, parts, half, lanes = x_refs[0].shape
    low = iota((half, lanes), 1) < ROWS
    table = jnp.concatenate([table_ref[...], table_ref[...]], axis=1)
    high, rest = split2(table)
    left = jnp.concatenate([high, rest], axis=1)
    width = 2 * half * len(x_refs)
    for source in range(sources):
        for part in range(parts):
            pieces = []
            for x_ref in x_refs:
                x = x_ref[source, part].astype(F32)
                pieces += [jnp.where(low, x, 0.0), jnp.where(low, 0.0, x)]
            both = jnp.concatenate(pieces, axis=0).astype(BF16)
            right = jnp.concatenate([both, both], axis=1)
            out_ref[part, :, source * width : (source + 1) * width] = lax.dot_general(
                left, right, (((1,), (1,)), ((), ())), preferred_element_type=F32
            )


def transform(*linked):
    sources, parts, half, _ = linked[0].shape
    return pl.pallas_call(
        dct_kernel,
        out_shape=jax.ShapeDtypeStruct((parts, ROWS, sources * 2 * half * len(linked)), F32),
        in_specs=[pl.BlockSpec(memory_space=pltpu.VMEM)] * (1 + len(linked)),
        out_specs=pl.BlockSpec(memory_space=pltpu.VMEM),
        name="transform",
    )(*in_vmem(dct_table(ROWS), *linked))


def exchange(blocks):
    return lax.all_to_all(blocks, "pix", split_axis=0, concat_axis=0, tiled=True)


def whole_dates(slcs, reference, strip_columns):
    devices = lax.axis_size("pix")
    width = strip_columns // devices
    chunk = width // CHUNKS
    arrived = [exchange(pack(slcs, k, CHUNKS, devices)) for k in range(CHUNKS)]
    sent, compressed = [], []
    for k in range(CHUNKS):
        linked, comp = link(arrived[k], reference, k * chunk, strip_columns)
        sent.append(exchange(linked))
        compressed.append(comp)
    return transform(*sent), jnp.concatenate(compressed, axis=2)


def parts_of_dates(slcs, reference, strip_columns):
    devices = lax.axis_size("pix")
    width = strip_columns // devices
    local_rows = slcs.shape[1]
    padded = jnp.pad(slcs, ((0, 0), (0, 0), (MARGIN, MARGIN)))
    blocks = jnp.stack(
        [padded[:, :, d * width : d * width + width + 2 * MARGIN] for d in range(devices)]
    )
    window = exchange(blocks)
    per_date = ROWS // local_rows
    window = window.reshape(DATES, per_date, 2, local_rows, width + 2 * MARGIN)
    z = window.transpose(0, 4, 2, 1, 3).reshape(DATES, width + 2 * MARGIN, 2 * ROWS)
    linked, compressed = link(z, reference, 0, strip_columns)
    linked = linked.astype(F32).reshape(DATES, 2, width // 2, 2, ROWS)
    spectrum = jnp.einsum(
        "qr,kpchr->kqphc", dct_table(ROWS), linked, precision=lax.Precision.HIGHEST
    ).reshape(DATES * ROWS // local_rows, local_rows, 2, width)
    arrived = exchange(spectrum.astype(BF16))
    spectrum = arrived.transpose(2, 1, 0, 3).reshape(2, local_rows, strip_columns)
    return spectrum.astype(F32), compressed


def on_device(slcs, ref_date):
    plan = whole_dates if slcs.shape[1] == ROWS else parts_of_dates
    return plan(slcs, ref_date, slcs.shape[2])


def solution(mesh):
    return jax.shard_map(
        on_device,
        mesh=mesh,
        in_specs=(P(None, ("grp", "pix"), None), P("grp")),
        out_specs=(P(None, ("grp", "pix"), None), P(None, None, ("grp", "pix"))),
        check_vma=False,
    )
```

```python
import functools
import math

import jax
import jax.numpy as jnp
from jax import lax
from jax.experimental import pallas as pl
from jax.experimental.pallas import tpu as pltpu
from jax.sharding import PartitionSpec as P

DATES = 16
ROWS = 64
HALF_X = 5
HALF_Y = 2
POWER_ITERS = 6
LOADING = 0.25

STEPS = 4
MARGIN = 8
TILE = 16
UNROLL = 4
GROUP = 4
PAIRS = DATES // 2
F32 = jnp.float32
BF16 = jnp.bfloat16
OUT = pltpu.VMEM


def iota(shape, dim):
    return lax.broadcasted_iota(jnp.int32, shape, dim)


def in_vmem(*arrays):
    return [pltpu.with_memory_space_constraint(x, pltpu.VMEM) for x in arrays]


def pack_kernel(x_hbm, out_hbm, x_ref, out_ref, in_sems, out_sems):
    devices, tall, _ = out_ref.shape
    width = tall - 2 * MARGIN
    steps = in_sems.shape[0]
    each = devices // steps

    def columns_in(step):
        at = slice(step * each * width, (step + 1) * each * width)
        return pltpu.make_async_copy(
            x_hbm.at[:, :, at], x_ref.at[:, :, at], in_sems.at[step]
        )

    def blocks_out(step):
        at = slice(step * each, (step + 1) * each)
        return pltpu.make_async_copy(out_ref.at[at], out_hbm.at[at], out_sems.at[step])

    for step in range(steps):
        columns_in(step).start()
    zero = jnp.zeros((MARGIN, out_ref.shape[2]), BF16)
    out_ref[0, 0:MARGIN, :] = zero
    out_ref[devices - 1, tall - MARGIN :, :] = zero
    for block in range(devices):
        if block % each == 0:
            columns_in(block // each).wait()
        columns = slice(block * width, (block + 1) * width)
        tile = jnp.concatenate([x_ref[0, :, columns], x_ref[1, :, columns]], axis=0)
        turned = tile.astype(F32).T.astype(BF16)
        out_ref[block, MARGIN : width + MARGIN, :] = turned
        if block > 0:
            out_ref[block - 1, width + MARGIN :, :] = turned[0:MARGIN]
        if block < devices - 1:
            out_ref[block + 1, 0:MARGIN, :] = turned[width - MARGIN :]
        if block % each == 0 and block > 0:
            blocks_out(block // each - 1).start()
    blocks_out(steps - 1).start()
    for step in range(steps):
        blocks_out(step).wait()


def pack(slcs, devices):
    parts, lines, columns = slcs.shape
    shape = (devices, columns // devices + 2 * MARGIN, parts * lines)
    steps = math.gcd(devices, STEPS)
    return pl.pallas_call(
        pack_kernel,
        out_shape=jax.ShapeDtypeStruct(shape, BF16),
        in_specs=[pl.BlockSpec(memory_space=pltpu.HBM)],
        out_specs=pl.BlockSpec(memory_space=pltpu.HBM),
        scratch_shapes=[
            pltpu.VMEM(slcs.shape, BF16),
            pltpu.VMEM(shape, BF16),
            pltpu.SemaphoreType.DMA((steps,)),
            pltpu.SemaphoreType.DMA((steps,)),
        ],
        name="pack",
    )(slcs)


def split2(x):
    high = x.astype(BF16)
    return high, (x - high.astype(F32)).astype(BF16)


def inverse_counts(first_column, strip_columns, half):
    shape = (half, 2 * ROWS)
    lane = iota(shape, 1)
    line = lane % ROWS
    column = first_column + iota(shape, 0) + (lane // ROWS) * half
    lines = jnp.minimum(line + HALF_Y, ROWS - 1) - jnp.maximum(line - HALF_Y, 0) + 1
    columns = (
        jnp.minimum(column + HALF_X, strip_columns - 1) - jnp.maximum(column - HALF_X, 0) + 1
    )
    return 1.0 / (lines * columns).astype(F32)


def tree(terms):
    while len(terms) > 1:
        terms = [
            terms[k] + terms[k + 1] if k + 1 < len(terms) else terms[k]
            for k in range(0, len(terms), 2)
        ]
    return terms[0]


def entry(i, j):
    offset = (j - i) % DATES
    if offset < PAIRS or (offset == PAIRS and i < j):
        return offset - 1, i, False
    return DATES - offset - 1, j, True


def packed(x):
    return x.astype(F32).astype(BF16)


def link_kernel(
    strip_columns,
    reference_ref,
    z_ref,
    linked_hbm,
    comp_ref,
    linked_ref,
    sems,
    window,
    center,
    summed_even,
    summed_odd,
    cov,
    diag,
    vec,
    narrow,
    comp,
):
    half = center.shape[2]
    tall = window.shape[2]
    lanes = 2 * ROWS
    reference = reference_ref[0]
    first_column = lax.axis_index("pix") * (strip_columns // lax.axis_size("pix"))

    low = iota((tall, lanes), 1) < ROWS

    def unmix(n, carry):
        for u in range(UNROLL):
            k = n * UNROLL + u
            top = z_ref[k, 0:tall, :].astype(F32)
            bottom = z_ref[k, half : half + tall, :].astype(F32)
            real = jnp.where(low, top, pltpu.roll(bottom, ROWS, 1))
            imag = jnp.where(low, pltpu.roll(top, ROWS, 1), bottom)
            window[k, 0] = real.astype(BF16)
            window[k, 1] = imag.astype(BF16)
            center[k, 0] = real[MARGIN : MARGIN + half]
            center[k, 1] = imag[MARGIN : MARGIN + half]
        return carry

    lax.fori_loop(0, DATES // UNROLL, unmix, 0)

    wide = 2 * lanes
    row, col = iota((wide, wide), 0), iota((wide, wide), 1)
    band_lines = jnp.where(
        (row // ROWS == col // ROWS) & (jnp.abs(row - col) <= HALF_Y), 1.0, 0.0
    ).astype(BF16)
    out_row, in_row = iota((half, tall), 0), iota((half, tall), 1)
    band_columns = jnp.where(jnp.abs(out_row + MARGIN - in_row) <= HALF_X, 1.0, 0.0).astype(BF16)
    inverse = inverse_counts(first_column, strip_columns, half)

    def offsets(i):
        return range(1, PAIRS + 1 if i < PAIRS else PAIRS)

    def sum_columns(i, slot, summed):
        real, imag = packed(window[i, 0]), packed(window[i, 1])
        real32, imag32 = real.astype(F32), imag.astype(F32)
        for offset in (0, *offsets(i)):
            if offset:
                j = (i + offset) % DATES
                real_j, imag_j = packed(window[j, 0]), packed(window[j, 1])
                left = real * real_j + imag * imag_j
                right = imag * real_j - real * imag_j
            else:
                left, right = split2(real32 * real32 + imag32 * imag32)
            sums = jnp.dot(
                band_columns,
                jnp.concatenate([left, right], axis=1),
                preferred_element_type=F32,
            )
            left, right = sums[:, 0:lanes], sums[:, lanes:]
            if offset:
                left, right = left.astype(BF16), right.astype(BF16)
            else:
                left, right = split2(left + right)
            at = (slot * len((0, *offsets(i))) + offset) * half
            summed[0, at : at + half] = left
            summed[1, at : at + half] = right

    def sum_lines(i, summed):
        count = len((0, *offsets(i)))
        used = slice(0, 2 * count * half)
        both = jnp.concatenate([packed(summed[0, used]), packed(summed[1, used])], axis=1)
        boxes = jnp.dot(both, band_lines, preferred_element_type=F32)
        for slot in range(2):
            for offset in (0, *offsets(i)):
                at = (slot * count + offset) * half
                box = boxes[at : at + half]
                if offset:
                    for part in range(2):
                        value = box[:, part * lanes : (part + 1) * lanes] * inverse
                        value = value.astype(BF16)
                        for g in range(half // TILE):
                            tile = value[g * TILE : (g + 1) * TILE]
                            cov[g, offset - 1, i + slot, part] = tile
                else:
                    value = (box[:, 0:lanes] + box[:, lanes:]) * inverse
                    value = value.astype(BF16).astype(F32) + LOADING
                    for g in range(half // TILE):
                        diag[g, i + slot] = value[g * TILE : (g + 1) * TILE]

    def columns_of_two(i, summed):
        for slot in range(2):
            sum_columns(i + slot, slot, summed)

    buffers = summed_even, summed_odd
    for n in range(DATES // 2 + 1):
        if n < DATES // 2:
            columns_of_two(2 * n, buffers[n % 2])
        if n > 0:
            sum_lines(2 * n - 2, buffers[(n - 1) % 2])

    def first_step(n, carry):
        for u in range(UNROLL):
            column_entry(n * UNROLL + u)
        return carry

    def column_entry(k):
        offset = (reference + DATES - k) % DATES
        plain = (offset < PAIRS) | ((offset == PAIRS) & (k < reference))
        slot = jnp.where(plain, jnp.maximum(offset, 1), DATES - offset) - 1
        date = jnp.where(plain, k, reference)
        sign = jnp.where(offset == 0, 0.0, jnp.where(plain, 1.0, -1.0)).astype(F32)
        for g in range(half // TILE):
            real = jnp.where(offset == 0, diag[g, k], cov[g, slot, date, 0].astype(F32))
            imag = cov[g, slot, date, 1].astype(F32) * sign
            vec[g, k, 0] = real
            vec[g, k, 1] = imag
            narrow[g, k, 0] = real.astype(BF16)
            narrow[g, k, 1] = imag.astype(BF16)

    lax.fori_loop(0, DATES // UNROLL, first_step, 0)

    def one_tile(g, carry):
        def step(last):
            real = [packed(narrow[g, k, 0]) for k in range(DATES)]
            imag = [packed(narrow[g, k, 1]) for k in range(DATES)]
            for i in range(DATES):
                own = diag[g, i]
                total = [own * vec[g, i, 0], own * vec[g, i, 1]]
                sums = [None, None]
                others = [j for j in range(DATES) if j != i]
                for at in range(0, len(others), GROUP):
                    terms = [], []
                    for j in others[at : at + GROUP]:
                        slot, date, conjugated = entry(i, j)
                        a = packed(cov[g, slot, date, 0])
                        b = packed(cov[g, slot, date, 1])
                        if conjugated:
                            terms[0].append(a * real[j] + b * imag[j])
                            terms[1].append(a * imag[j] - b * real[j])
                        else:
                            terms[0].append(a * real[j] - b * imag[j])
                            terms[1].append(a * imag[j] + b * real[j])
                    for part in range(2):
                        term = tree(terms[part])
                        if last:
                            total[part] = total[part] + term.astype(F32)
                        else:
                            sums[part] = term if at == 0 else sums[part] + term
                for part in range(2):
                    if not last:
                        total[part] = total[part] + sums[part].astype(F32)
                        narrow[g, i, part] = total[part].astype(BF16)
                    vec[g, i, part] = total[part]

        def early_step(t, carry):
            step(False)
            return carry

        lax.fori_loop(0, POWER_ITERS - 2, early_step, 0)
        step(True)

        for sub in range(0, TILE, 8):
            at = slice(sub, sub + 8)
            rows = pl.ds(pl.multiple_of(g * TILE + sub, 8), 8)
            squares = []
            for k in range(DATES):
                real, imag = vec[g, k, 0, at], vec[g, k, 1, at]
                squares.append(real * real + imag * imag)
            scale = DATES / tree(squares)
            ref_real = vec[g, reference, 0, at] * scale
            ref_imag = vec[g, reference, 1, at] * scale
            comp_real = comp_imag = None
            for k in range(DATES):
                real, imag = vec[g, k, 0, at], vec[g, k, 1, at]
                linked_real = real * ref_real + imag * ref_imag
                linked_imag = imag * ref_real - real * ref_imag
                z_real, z_imag = center[k, 0, rows, :], center[k, 1, rows, :]
                more_real = linked_real * z_real + linked_imag * z_imag
                more_imag = linked_real * z_imag - linked_imag * z_real
                comp_real = more_real if k == 0 else comp_real + more_real
                comp_imag = more_imag if k == 0 else comp_imag + more_imag
                linked_ref[g, k, 0, at] = linked_real.astype(BF16)
                linked_ref[g, k, 1, at] = linked_imag.astype(BF16)
            comp[0, rows, :] = comp_real * (1.0 / math.sqrt(DATES))
            comp[1, rows, :] = comp_imag * (1.0 / math.sqrt(DATES))
        tile_out(g).start()
        return carry

    def tile_out(g):
        rows = pl.ds(pl.multiple_of(g * TILE, TILE), TILE)
        return pltpu.make_async_copy(
            linked_ref.at[g], linked_hbm.at[:, :, rows, :], sems.at[g]
        )

    lax.fori_loop(0, half // TILE, one_tile, 0)

    for part in range(2):
        turned = comp[part].T
        comp_ref[part] = jnp.concatenate([turned[0:ROWS], turned[ROWS:]], axis=1)
    for g in range(half // TILE):
        tile_out(g).wait()


def link(z, reference, strip_columns):
    width = z.shape[1] - 2 * MARGIN
    half = width // 2
    tall = half + 2 * MARGIN
    lanes = 2 * ROWS
    return pl.pallas_call(
        functools.partial(link_kernel, strip_columns),
        out_shape=(
            jax.ShapeDtypeStruct((DATES, 2, half, lanes), BF16),
            OUT((2, ROWS, width), F32),
        ),
        in_specs=[
            pl.BlockSpec(memory_space=pltpu.SMEM),
            pl.BlockSpec(memory_space=pltpu.VMEM),
        ],
        out_specs=(
            pl.BlockSpec(memory_space=pltpu.HBM),
            pl.BlockSpec(memory_space=pltpu.VMEM),
        ),
        scratch_shapes=[
            pltpu.VMEM((half // TILE, DATES, 2, TILE, lanes), BF16),
            pltpu.SemaphoreType.DMA((half // TILE,)),
            pltpu.VMEM((DATES, 2, tall, lanes), BF16),
            pltpu.VMEM((DATES, 2, half, lanes), F32),
            pltpu.VMEM((2, 2 * (PAIRS + 1) * half, lanes), BF16),
            pltpu.VMEM((2, 2 * (PAIRS + 1) * half, lanes), BF16),
            pltpu.VMEM((half // TILE, PAIRS, DATES, 2, TILE, lanes), BF16),
            pltpu.VMEM((half // TILE, DATES, TILE, lanes), F32),
            pltpu.VMEM((half // TILE, DATES, 2, TILE, lanes), F32),
            pltpu.VMEM((half // TILE, DATES, 2, TILE, lanes), BF16),
            pltpu.VMEM((2, half, lanes), F32),
        ],
        cost_estimate=pl.CostEstimate(
            flops=16 * DATES * DATES * POWER_ITERS * width * ROWS,
            bytes_accessed=6 * DATES * width * ROWS,
            transcendentals=0,
        ),
        name="link",
    )(reference, *in_vmem(z))


def dct_table(line_count):
    frequency = jnp.arange(line_count, dtype=F32)[:, None]
    position = jnp.arange(line_count, dtype=F32)[None, :]
    weight = jnp.where(frequency == 0, math.sqrt(1.0 / line_count), math.sqrt(2.0 / line_count))
    return weight * jnp.cos(jnp.pi * (2.0 * position + 1.0) * frequency / (2.0 * line_count))


def dct_kernel(table_ref, x_ref, out_hbm, out_ref, sems):
    sources, parts, half, lanes = x_ref.shape
    low = iota((half, lanes), 1) < ROWS
    table = jnp.concatenate([table_ref[...], table_ref[...]], axis=1)
    high, rest = split2(table)
    left = jnp.concatenate([high, rest], axis=1)
    width = 2 * half
    steps = sems.shape[0]
    each = sources // steps

    def columns_out(step):
        at = slice(step * each * width, (step + 1) * each * width)
        return pltpu.make_async_copy(
            out_ref.at[:, :, at], out_hbm.at[:, :, at], sems.at[step]
        )

    for source in range(sources):
        for part in range(parts):
            x = x_ref[source, part].astype(F32)
            both = jnp.concatenate([jnp.where(low, x, 0.0), jnp.where(low, 0.0, x)], axis=0)
            both = both.astype(BF16)
            right = jnp.concatenate([both, both], axis=1)
            out_ref[part, :, source * width : (source + 1) * width] = lax.dot_general(
                left, right, (((1,), (1,)), ((), ())), preferred_element_type=F32
            )
        if source % each == each - 1:
            columns_out(source // each).start()
    for step in range(steps):
        columns_out(step).wait()


def transform(linked):
    sources, parts, half, _ = linked.shape
    shape = (parts, ROWS, sources * 2 * half)
    return pl.pallas_call(
        dct_kernel,
        out_shape=jax.ShapeDtypeStruct(shape, F32),
        in_specs=[pl.BlockSpec(memory_space=pltpu.VMEM)] * 2,
        out_specs=pl.BlockSpec(memory_space=pltpu.HBM),
        scratch_shapes=[
            pltpu.VMEM(shape, F32),
            pltpu.SemaphoreType.DMA((math.gcd(sources, STEPS),)),
        ],
        name="transform",
    )(*in_vmem(dct_table(ROWS), linked))


def exchange(blocks):
    return lax.all_to_all(blocks, "pix", split_axis=0, concat_axis=0, tiled=True)


def whole_dates(slcs, reference, strip_columns):
    arrived = exchange(pack(slcs, lax.axis_size("pix")))
    linked, compressed = link(arrived, reference, strip_columns)
    return transform(exchange(linked)), compressed


def parts_of_dates(slcs, reference, strip_columns):
    devices = lax.axis_size("pix")
    width = strip_columns // devices
    local_rows = slcs.shape[1]
    padded = jnp.pad(slcs, ((0, 0), (0, 0), (MARGIN, MARGIN)))
    blocks = jnp.stack(
        [padded[:, :, d * width : d * width + width + 2 * MARGIN] for d in range(devices)]
    )
    window = exchange(blocks)
    per_date = ROWS // local_rows
    window = window.reshape(DATES, per_date, 2, local_rows, width + 2 * MARGIN)
    z = window.transpose(0, 4, 2, 1, 3).reshape(DATES, width + 2 * MARGIN, 2 * ROWS)
    linked, compressed = link(z, reference, strip_columns)
    linked = linked.astype(F32).reshape(DATES, 2, width // 2, 2, ROWS)
    spectrum = jnp.einsum(
        "qr,kpchr->kqphc", dct_table(ROWS), linked, precision=lax.Precision.HIGHEST
    ).reshape(DATES * ROWS // local_rows, local_rows, 2, width)
    arrived = exchange(spectrum.astype(BF16))
    spectrum = arrived.transpose(2, 1, 0, 3).reshape(2, local_rows, strip_columns)
    return spectrum.astype(F32), compressed


def on_device(slcs, ref_date):
    plan = whole_dates if slcs.shape[1] == ROWS else parts_of_dates
    return plan(slcs, ref_date, slcs.shape[2])


def solution(mesh):
    return jax.shard_map(
        on_device,
        mesh=mesh,
        in_specs=(P(None, ("grp", "pix"), None), P("grp")),
        out_specs=(P(None, ("grp", "pix"), None), P(None, None, ("grp", "pix"))),
        check_vma=False,
    )
```

```python
import functools
import math

import jax
import jax.numpy as jnp
from jax import lax
from jax.experimental import pallas as pl
from jax.experimental.pallas import tpu as pltpu
from jax.sharding import PartitionSpec as P

DATES = 16
ROWS = 64
HALF_X = 5
HALF_Y = 2
POWER_ITERS = 6
LOADING = 0.25

STEPS = 4
MARGIN = 8
TILE = 16
UNROLL = 4
GROUP = 4
PAIRS = DATES // 2
F32 = jnp.float32
BF16 = jnp.bfloat16
OUT = pltpu.VMEM


def iota(shape, dim):
    return lax.broadcasted_iota(jnp.int32, shape, dim)


def in_vmem(*arrays):
    return [pltpu.with_memory_space_constraint(x, pltpu.VMEM) for x in arrays]


def pack_kernel(x_hbm, out_hbm, x_ref, out_ref, in_sems, out_sems):
    devices, tall, _ = out_ref.shape
    width = tall - 2 * MARGIN
    steps = in_sems.shape[0]
    each = devices // steps

    def columns_in(step):
        at = slice(step * each * width, (step + 1) * each * width)
        return pltpu.make_async_copy(
            x_hbm.at[:, :, at], x_ref.at[:, :, at], in_sems.at[step]
        )

    def blocks_out(step):
        at = slice(step * each, (step + 1) * each)
        return pltpu.make_async_copy(out_ref.at[at], out_hbm.at[at], out_sems.at[step])

    for step in range(steps):
        columns_in(step).start()
    zero = jnp.zeros((MARGIN, out_ref.shape[2]), BF16)
    out_ref[0, 0:MARGIN, :] = zero
    out_ref[devices - 1, tall - MARGIN :, :] = zero
    for block in range(devices):
        if block % each == 0:
            columns_in(block // each).wait()
        columns = slice(block * width, (block + 1) * width)
        tile = jnp.concatenate([x_ref[0, :, columns], x_ref[1, :, columns]], axis=0)
        turned = tile.T
        out_ref[block, MARGIN : width + MARGIN, :] = turned
        if block > 0:
            out_ref[block - 1, width + MARGIN :, :] = turned[0:MARGIN]
        if block < devices - 1:
            out_ref[block + 1, 0:MARGIN, :] = turned[width - MARGIN :]
        if block % each == 0 and block > 0:
            blocks_out(block // each - 1).start()
    blocks_out(steps - 1).start()
    for step in range(steps):
        blocks_out(step).wait()


def pack(slcs, devices):
    parts, lines, columns = slcs.shape
    shape = (devices, columns // devices + 2 * MARGIN, parts * lines)
    steps = math.gcd(devices, STEPS)
    return pl.pallas_call(
        pack_kernel,
        out_shape=jax.ShapeDtypeStruct(shape, BF16),
        in_specs=[pl.BlockSpec(memory_space=pltpu.HBM)],
        out_specs=pl.BlockSpec(memory_space=pltpu.HBM),
        scratch_shapes=[
            pltpu.VMEM(slcs.shape, BF16),
            pltpu.VMEM(shape, BF16),
            pltpu.SemaphoreType.DMA((steps,)),
            pltpu.SemaphoreType.DMA((steps,)),
        ],
        name="pack",
    )(slcs)


def split2(x):
    high = x.astype(BF16)
    return high, (x - high.astype(F32)).astype(BF16)


def inverse_counts(first_column, strip_columns, half):
    shape = (half, 2 * ROWS)
    lane = iota(shape, 1)
    line = lane % ROWS
    column = first_column + iota(shape, 0) + (lane // ROWS) * half
    lines = jnp.minimum(line + HALF_Y, ROWS - 1) - jnp.maximum(line - HALF_Y, 0) + 1
    columns = (
        jnp.minimum(column + HALF_X, strip_columns - 1) - jnp.maximum(column - HALF_X, 0) + 1
    )
    return 1.0 / (lines * columns).astype(F32)


def tree(terms):
    while len(terms) > 1:
        terms = [
            terms[k] + terms[k + 1] if k + 1 < len(terms) else terms[k]
            for k in range(0, len(terms), 2)
        ]
    return terms[0]


def entry(i, j):
    offset = (j - i) % DATES
    if offset < PAIRS or (offset == PAIRS and i < j):
        return offset - 1, i, False
    return DATES - offset - 1, j, True


def packed(x):
    return x.astype(F32).astype(BF16)


def link_kernel(
    strip_columns,
    reference_ref,
    z_ref,
    linked_hbm,
    comp_ref,
    linked_ref,
    sems,
    window,
    center,
    summed_even,
    summed_odd,
    cov,
    diag,
    vec,
    narrow,
    comp,
):
    half = center.shape[2]
    tall = window.shape[2]
    lanes = 2 * ROWS
    reference = reference_ref[0]
    first_column = lax.axis_index("pix") * (strip_columns // lax.axis_size("pix"))

    low = iota((tall, lanes), 1) < ROWS

    def unmix(k):
        top = z_ref[k, 0:tall, :].astype(F32)
        bottom = z_ref[k, half : half + tall, :].astype(F32)
        real = jnp.where(low, top, pltpu.roll(bottom, ROWS, 1))
        imag = jnp.where(low, pltpu.roll(top, ROWS, 1), bottom)
        window[k, 0] = real.astype(BF16)
        window[k, 1] = imag.astype(BF16)
        center[k, 0] = real[MARGIN : MARGIN + half]
        center[k, 1] = imag[MARGIN : MARGIN + half]

    wide = 2 * lanes
    row, col = iota((wide, wide), 0), iota((wide, wide), 1)
    band_lines = jnp.where(
        (row // ROWS == col // ROWS) & (jnp.abs(row - col) <= HALF_Y), 1.0, 0.0
    ).astype(BF16)
    out_row, in_row = iota((half, tall), 0), iota((half, tall), 1)
    band_columns = jnp.where(jnp.abs(out_row + MARGIN - in_row) <= HALF_X, 1.0, 0.0).astype(BF16)
    inverse = inverse_counts(first_column, strip_columns, half)

    def offsets(i):
        return range(1, PAIRS + 1 if i < PAIRS else PAIRS)

    def sum_columns(i, slot, summed):
        real, imag = packed(window[i, 0]), packed(window[i, 1])
        real32, imag32 = real.astype(F32), imag.astype(F32)
        for offset in (0, *offsets(i)):
            if offset:
                j = (i + offset) % DATES
                real_j, imag_j = packed(window[j, 0]), packed(window[j, 1])
                left = real * real_j + imag * imag_j
                right = imag * real_j - real * imag_j
            else:
                left, right = split2(real32 * real32 + imag32 * imag32)
            sums = jnp.dot(
                band_columns,
                jnp.concatenate([left, right], axis=1),
                preferred_element_type=F32,
            )
            left, right = sums[:, 0:lanes], sums[:, lanes:]
            if offset:
                left, right = left.astype(BF16), right.astype(BF16)
            else:
                left, right = split2(left + right)
            at = (slot * len((0, *offsets(i))) + offset) * half
            summed[0, at : at + half] = left
            summed[1, at : at + half] = right

    def sum_lines(i, summed):
        count = len((0, *offsets(i)))
        used = slice(0, 2 * count * half)
        both = jnp.concatenate([packed(summed[0, used]), packed(summed[1, used])], axis=1)
        boxes = jnp.dot(both, band_lines, preferred_element_type=F32)
        for slot in range(2):
            for offset in (0, *offsets(i)):
                at = (slot * count + offset) * half
                box = boxes[at : at + half]
                if offset:
                    for part in range(2):
                        value = box[:, part * lanes : (part + 1) * lanes] * inverse
                        value = value.astype(BF16)
                        for g in range(half // TILE):
                            tile = value[g * TILE : (g + 1) * TILE]
                            cov[g, offset - 1, i + slot, part] = tile
                else:
                    value = (box[:, 0:lanes] + box[:, lanes:]) * inverse
                    value = value.astype(BF16).astype(F32) + LOADING
                    for g in range(half // TILE):
                        diag[g, i + slot] = value[g * TILE : (g + 1) * TILE]

    def columns_of_two(i, summed):
        for slot in range(2):
            sum_columns(i + slot, slot, summed)

    buffers = summed_even, summed_odd
    ready = 0
    for n in range(DATES // 2 + 1):
        if n < DATES // 2:
            while ready < min(2 * n + 2 + PAIRS, DATES):
                unmix(ready)
                ready += 1
            columns_of_two(2 * n, buffers[n % 2])
        if n > 0:
            sum_lines(2 * n - 2, buffers[(n - 1) % 2])

    def first_step(n, carry):
        for u in range(UNROLL):
            column_entry(n * UNROLL + u)
        return carry

    def column_entry(k):
        offset = (reference + DATES - k) % DATES
        plain = (offset < PAIRS) | ((offset == PAIRS) & (k < reference))
        slot = jnp.where(plain, jnp.maximum(offset, 1), DATES - offset) - 1
        date = jnp.where(plain, k, reference)
        sign = jnp.where(offset == 0, 0.0, jnp.where(plain, 1.0, -1.0)).astype(F32)
        for g in range(half // TILE):
            real = jnp.where(offset == 0, diag[g, k], cov[g, slot, date, 0].astype(F32))
            imag = cov[g, slot, date, 1].astype(F32) * sign
            vec[g, k, 0] = real
            vec[g, k, 1] = imag
            narrow[g, k, 0] = real.astype(BF16)
            narrow[g, k, 1] = imag.astype(BF16)

    lax.fori_loop(0, DATES // UNROLL, first_step, 0)

    def one_tile(g, carry):
        def step(last):
            real = [packed(narrow[g, k, 0]) for k in range(DATES)]
            imag = [packed(narrow[g, k, 1]) for k in range(DATES)]
            for i in range(DATES):
                own = diag[g, i]
                total = [own * vec[g, i, 0], own * vec[g, i, 1]]
                sums = [None, None]
                others = [j for j in range(DATES) if j != i]
                for at in range(0, len(others), GROUP):
                    terms = [], []
                    for j in others[at : at + GROUP]:
                        slot, date, conjugated = entry(i, j)
                        a = packed(cov[g, slot, date, 0])
                        b = packed(cov[g, slot, date, 1])
                        if conjugated:
                            terms[0].append(a * real[j] + b * imag[j])
                            terms[1].append(a * imag[j] - b * real[j])
                        else:
                            terms[0].append(a * real[j] - b * imag[j])
                            terms[1].append(a * imag[j] + b * real[j])
                    for part in range(2):
                        term = tree(terms[part])
                        if last:
                            total[part] = total[part] + term.astype(F32)
                        else:
                            sums[part] = term if at == 0 else sums[part] + term
                for part in range(2):
                    if not last:
                        total[part] = total[part] + sums[part].astype(F32)
                        narrow[g, i, part] = total[part].astype(BF16)
                    vec[g, i, part] = total[part]

        def early_step(t, carry):
            step(False)
            return carry

        lax.fori_loop(0, POWER_ITERS - 2, early_step, 0)
        step(True)

        for sub in range(0, TILE, 8):
            at = slice(sub, sub + 8)
            rows = pl.ds(pl.multiple_of(g * TILE + sub, 8), 8)
            left_half = iota((8, lanes), 1) < ROWS
            squares = []
            for k in range(DATES):
                real, imag = vec[g, k, 0, at], vec[g, k, 1, at]
                squares.append(real * real + imag * imag)
            scale = DATES / tree(squares)
            ref_real = vec[g, reference, 0, at] * scale
            ref_imag = vec[g, reference, 1, at] * scale
            comp_real = comp_imag = None
            for k in range(DATES):
                real, imag = vec[g, k, 0, at], vec[g, k, 1, at]
                linked_real = real * ref_real + imag * ref_imag
                linked_imag = imag * ref_real - real * ref_imag
                z_real, z_imag = center[k, 0, rows, :], center[k, 1, rows, :]
                more_real = linked_real * z_real + linked_imag * z_imag
                more_imag = linked_real * z_imag - linked_imag * z_real
                comp_real = more_real if k == 0 else comp_real + more_real
                comp_imag = more_imag if k == 0 else comp_imag + more_imag
                first = jnp.where(left_half, linked_real, pltpu.roll(linked_imag, ROWS, 1))
                second = jnp.where(left_half, pltpu.roll(linked_real, ROWS, 1), linked_imag)
                linked_ref[g, k, 0, at] = first.astype(BF16)
                linked_ref[g, k, 1, at] = second.astype(BF16)
            comp[0, rows, :] = comp_real * (1.0 / math.sqrt(DATES))
            comp[1, rows, :] = comp_imag * (1.0 / math.sqrt(DATES))
        tile_out(g).start()
        return carry

    def tile_out(g):
        rows = pl.ds(pl.multiple_of(g * TILE, TILE), TILE)
        return pltpu.make_async_copy(
            linked_ref.at[g], linked_hbm.at[:, :, rows, :], sems.at[g]
        )

    lax.fori_loop(0, half // TILE, one_tile, 0)

    for part in range(2):
        turned = comp[part].T
        comp_ref[part] = jnp.concatenate([turned[0:ROWS], turned[ROWS:]], axis=1)
    for g in range(half // TILE):
        tile_out(g).wait()


def link(z, reference, strip_columns):
    width = z.shape[1] - 2 * MARGIN
    half = width // 2
    tall = half + 2 * MARGIN
    lanes = 2 * ROWS
    return pl.pallas_call(
        functools.partial(link_kernel, strip_columns),
        out_shape=(
            jax.ShapeDtypeStruct((DATES, 2, half, lanes), BF16),
            OUT((2, ROWS, width), F32),
        ),
        in_specs=[
            pl.BlockSpec(memory_space=pltpu.SMEM),
            pl.BlockSpec(memory_space=pltpu.VMEM),
        ],
        out_specs=(
            pl.BlockSpec(memory_space=pltpu.HBM),
            pl.BlockSpec(memory_space=pltpu.VMEM),
        ),
        scratch_shapes=[
            pltpu.VMEM((half // TILE, DATES, 2, TILE, lanes), BF16),
            pltpu.SemaphoreType.DMA((half // TILE,)),
            pltpu.VMEM((DATES, 2, tall, lanes), BF16),
            pltpu.VMEM((DATES, 2, half, lanes), F32),
            pltpu.VMEM((2, 2 * (PAIRS + 1) * half, lanes), BF16),
            pltpu.VMEM((2, 2 * (PAIRS + 1) * half, lanes), BF16),
            pltpu.VMEM((half // TILE, PAIRS, DATES, 2, TILE, lanes), BF16),
            pltpu.VMEM((half // TILE, DATES, TILE, lanes), F32),
            pltpu.VMEM((half // TILE, DATES, 2, TILE, lanes), F32),
            pltpu.VMEM((half // TILE, DATES, 2, TILE, lanes), BF16),
            pltpu.VMEM((2, half, lanes), F32),
        ],
        cost_estimate=pl.CostEstimate(
            flops=16 * DATES * DATES * POWER_ITERS * width * ROWS,
            bytes_accessed=6 * DATES * width * ROWS,
            transcendentals=0,
        ),
        name="link",
    )(reference, *in_vmem(z))


def dct_table(line_count):
    frequency = jnp.arange(line_count, dtype=F32)[:, None]
    position = jnp.arange(line_count, dtype=F32)[None, :]
    weight = jnp.where(frequency == 0, math.sqrt(1.0 / line_count), math.sqrt(2.0 / line_count))
    return weight * jnp.cos(jnp.pi * (2.0 * position + 1.0) * frequency / (2.0 * line_count))


def dct_kernel(table_ref, x_ref, out_hbm, out_ref, sems):
    sources, width, lanes = x_ref.shape
    high, rest = split2(table_ref[...])
    zero = jnp.zeros_like(high)
    left = jnp.concatenate(
        [
            jnp.concatenate([high, zero, rest, zero], axis=1),
            jnp.concatenate([zero, high, zero, rest], axis=1),
        ],
        axis=0,
    )
    steps = sems.shape[0]
    each = sources // steps

    def columns_out(step):
        at = slice(step * each * width, (step + 1) * each * width)
        return pltpu.make_async_copy(
            out_ref.at[:, :, at], out_hbm.at[:, :, at], sems.at[step]
        )

    for source in range(0, sources, 2):
        x = jnp.concatenate([x_ref[source], x_ref[source + 1]], axis=0)
        result = lax.dot_general(
            left,
            jnp.concatenate([x, x], axis=1),
            (((1,), (1,)), ((), ())),
            preferred_element_type=F32,
        )
        columns = slice(source * width, (source + 2) * width)
        out_ref[0, :, columns] = result[0:ROWS]
        out_ref[1, :, columns] = result[ROWS:]
        if (source + 2) % each == 0:
            columns_out((source + 2) // each - 1).start()
    for step in range(steps):
        columns_out(step).wait()


def transform(linked):
    sources, width, _ = linked.shape
    shape = (2, ROWS, sources * width)
    return pl.pallas_call(
        dct_kernel,
        out_shape=jax.ShapeDtypeStruct(shape, F32),
        in_specs=[pl.BlockSpec(memory_space=pltpu.VMEM)] * 2,
        out_specs=pl.BlockSpec(memory_space=pltpu.HBM),
        scratch_shapes=[
            pltpu.VMEM(shape, F32),
            pltpu.SemaphoreType.DMA((math.gcd(sources // 2, STEPS),)),
        ],
        name="transform",
    )(*in_vmem(dct_table(ROWS), linked))


def exchange(blocks):
    return lax.all_to_all(blocks, "pix", split_axis=0, concat_axis=0, tiled=True)


def whole_dates(slcs, reference, strip_columns):
    arrived = exchange(pack(slcs, lax.axis_size("pix")))
    linked, compressed = link(arrived, reference, strip_columns)
    arrived = exchange(linked)
    return transform(arrived.reshape(arrived.shape[0], -1, 2 * ROWS)), compressed


def parts_of_dates(slcs, reference, strip_columns):
    devices = lax.axis_size("pix")
    width = strip_columns // devices
    local_rows = slcs.shape[1]
    padded = jnp.pad(slcs, ((0, 0), (0, 0), (MARGIN, MARGIN)))
    blocks = jnp.stack(
        [padded[:, :, d * width : d * width + width + 2 * MARGIN] for d in range(devices)]
    )
    window = exchange(blocks)
    per_date = ROWS // local_rows
    window = window.reshape(DATES, per_date, 2, local_rows, width + 2 * MARGIN)
    z = window.transpose(0, 4, 2, 1, 3).reshape(DATES, width + 2 * MARGIN, 2 * ROWS)
    linked, compressed = link(z, reference, strip_columns)
    linked = linked.astype(F32).reshape(DATES, width, 2, ROWS)
    spectrum = jnp.einsum(
        "qr,kcpr->kqpc", dct_table(ROWS), linked, precision=lax.Precision.HIGHEST
    ).reshape(DATES * ROWS // local_rows, local_rows, 2, width)
    arrived = exchange(spectrum.astype(BF16))
    spectrum = arrived.transpose(2, 1, 0, 3).reshape(2, local_rows, strip_columns)
    return spectrum.astype(F32), compressed


def on_device(slcs, ref_date):
    plan = whole_dates if slcs.shape[1] == ROWS else parts_of_dates
    return plan(slcs, ref_date, slcs.shape[2])


def solution(mesh):
    return jax.shard_map(
        on_device,
        mesh=mesh,
        in_specs=(P(None, ("grp", "pix"), None), P("grp")),
        out_specs=(P(None, ("grp", "pix"), None), P(None, None, ("grp", "pix"))),
        check_vma=False,
    )
```

```python
import functools
import math

import jax
import jax.numpy as jnp
from jax import lax
from jax.experimental import pallas as pl
from jax.experimental.pallas import tpu as pltpu
from jax.sharding import PartitionSpec as P

DATES = 16
ROWS = 64
HALF_X = 5
HALF_Y = 2
POWER_ITERS = 6
LOADING = 0.25

STEPS = 4
MARGIN = 8
TILE = 16
UNROLL = 4
GROUP = 4
PAIRS = DATES // 2
F32 = jnp.float32
BF16 = jnp.bfloat16


def iota(shape, dim):
    return lax.broadcasted_iota(jnp.int32, shape, dim)


def in_vmem(*arrays):
    return [pltpu.with_memory_space_constraint(x, pltpu.VMEM) for x in arrays]


def pack_kernel(x_hbm, out_hbm, x_ref, out_ref, in_sems, out_sems):
    devices, tall, _ = out_ref.shape
    width = tall - 2 * MARGIN
    steps = in_sems.shape[0]
    each = devices // steps

    def columns_in(step):
        at = slice(step * each * width, (step + 1) * each * width)
        return pltpu.make_async_copy(
            x_hbm.at[:, :, at], x_ref.at[:, :, at], in_sems.at[step]
        )

    def blocks_out(step):
        at = slice(step * each, (step + 1) * each)
        return pltpu.make_async_copy(out_ref.at[at], out_hbm.at[at], out_sems.at[step])

    for step in range(steps):
        columns_in(step).start()
    zero = jnp.zeros((MARGIN, out_ref.shape[2]), BF16)
    out_ref[0, 0:MARGIN, :] = zero
    out_ref[devices - 1, tall - MARGIN :, :] = zero
    for block in range(devices):
        if block % each == 0:
            columns_in(block // each).wait()
        columns = slice(block * width, (block + 1) * width)
        tile = jnp.concatenate([x_ref[0, :, columns], x_ref[1, :, columns]], axis=0)
        turned = tile.T
        out_ref[block, MARGIN : width + MARGIN, :] = turned
        if block > 0:
            out_ref[block - 1, width + MARGIN :, :] = turned[0:MARGIN]
        if block < devices - 1:
            out_ref[block + 1, 0:MARGIN, :] = turned[width - MARGIN :]
        if block % each == 0 and block > 0:
            blocks_out(block // each - 1).start()
    blocks_out(steps - 1).start()
    for step in range(steps):
        blocks_out(step).wait()


def pack(slcs, devices):
    parts, lines, columns = slcs.shape
    shape = (devices, columns // devices + 2 * MARGIN, parts * lines)
    steps = math.gcd(devices, STEPS)
    return pl.pallas_call(
        pack_kernel,
        out_shape=jax.ShapeDtypeStruct(shape, BF16),
        in_specs=[pl.BlockSpec(memory_space=pltpu.HBM)],
        out_specs=pl.BlockSpec(memory_space=pltpu.HBM),
        scratch_shapes=[
            pltpu.VMEM(slcs.shape, BF16),
            pltpu.VMEM(shape, BF16),
            pltpu.SemaphoreType.DMA((steps,)),
            pltpu.SemaphoreType.DMA((steps,)),
        ],
        name="pack",
    )(slcs)


def split2(x):
    high = x.astype(BF16)
    return high, (x - high.astype(F32)).astype(BF16)


def inverse_counts(first_column, strip_columns, half):
    shape = (half, 2 * ROWS)
    lane = iota(shape, 1)
    line = lane % ROWS
    column = first_column + iota(shape, 0) + (lane // ROWS) * half
    lines = jnp.minimum(line + HALF_Y, ROWS - 1) - jnp.maximum(line - HALF_Y, 0) + 1
    columns = (
        jnp.minimum(column + HALF_X, strip_columns - 1) - jnp.maximum(column - HALF_X, 0) + 1
    )
    return 1.0 / (lines * columns).astype(F32)


def tree(terms):
    while len(terms) > 1:
        terms = [
            terms[k] + terms[k + 1] if k + 1 < len(terms) else terms[k]
            for k in range(0, len(terms), 2)
        ]
    return terms[0]


def entry(i, j):
    offset = (j - i) % DATES
    if offset < PAIRS or (offset == PAIRS and i < j):
        return offset - 1, i, False
    return DATES - offset - 1, j, True


def packed(x):
    return x.astype(F32).astype(BF16)


def link_kernel(
    strip_columns,
    reference_ref,
    z_ref,
    linked_hbm,
    linked_ref,
    sems,
    window,
    summed_even,
    summed_odd,
    cov,
    diag,
    vec,
    narrow,
):
    tall = window.shape[2]
    half = tall - 2 * MARGIN
    lanes = 2 * ROWS
    reference = reference_ref[0]
    first_column = lax.axis_index("pix") * (strip_columns // lax.axis_size("pix"))

    low = iota((tall, lanes), 1) < ROWS

    unmixed = set()

    def unmix(k):
        if k in unmixed:
            return
        unmixed.add(k)
        top = packed(z_ref[k, 0:tall, :])
        bottom = packed(z_ref[k, half : half + tall, :])
        window[k, 0] = jnp.where(low, top, pltpu.roll(bottom, ROWS, 1))
        window[k, 1] = jnp.where(low, pltpu.roll(top, ROWS, 1), bottom)

    wide = 2 * lanes
    row, col = iota((wide, wide), 0), iota((wide, wide), 1)
    band_lines = jnp.where(
        (row // ROWS == col // ROWS) & (jnp.abs(row - col) <= HALF_Y), 1.0, 0.0
    ).astype(BF16)
    out_row, in_row = iota((half, tall), 0), iota((half, tall), 1)
    band_columns = jnp.where(jnp.abs(out_row + MARGIN - in_row) <= HALF_X, 1.0, 0.0).astype(BF16)
    inverse = inverse_counts(first_column, strip_columns, half)

    def offsets(i):
        return range(1, PAIRS + 1 if i < PAIRS else PAIRS)

    def sum_columns(i, slot, summed):
        unmix(i)
        real, imag = packed(window[i, 0]), packed(window[i, 1])
        real32, imag32 = real.astype(F32), imag.astype(F32)
        for offset in (0, *offsets(i)):
            if offset:
                j = (i + offset) % DATES
                unmix(j)
                real_j, imag_j = packed(window[j, 0]), packed(window[j, 1])
                left = real * real_j + imag * imag_j
                right = imag * real_j - real * imag_j
            else:
                left, right = split2(real32 * real32 + imag32 * imag32)
            sums = jnp.dot(
                band_columns,
                jnp.concatenate([left, right], axis=1),
                preferred_element_type=F32,
            )
            left, right = sums[:, 0:lanes], sums[:, lanes:]
            if offset:
                left, right = left.astype(BF16), right.astype(BF16)
            else:
                left, right = split2(left + right)
            at = (slot * len((0, *offsets(i))) + offset) * half
            summed[0, at : at + half] = left
            summed[1, at : at + half] = right

    def sum_lines(i, summed):
        count = len((0, *offsets(i)))
        used = slice(0, 2 * count * half)
        both = jnp.concatenate([packed(summed[0, used]), packed(summed[1, used])], axis=1)
        boxes = jnp.dot(both, band_lines, preferred_element_type=F32)
        for slot in range(2):
            for offset in (0, *offsets(i)):
                at = (slot * count + offset) * half
                box = boxes[at : at + half]
                if offset:
                    for part in range(2):
                        value = box[:, part * lanes : (part + 1) * lanes] * inverse
                        value = value.astype(BF16)
                        for g in range(half // TILE):
                            tile = value[g * TILE : (g + 1) * TILE]
                            cov[g, offset - 1, i + slot, part] = tile
                else:
                    value = (box[:, 0:lanes] + box[:, lanes:]) * inverse
                    value = value.astype(BF16).astype(F32) + LOADING
                    for g in range(half // TILE):
                        diag[g, i + slot] = value[g * TILE : (g + 1) * TILE]

    def columns_of_two(i, summed):
        for slot in range(2):
            sum_columns(i + slot, slot, summed)

    buffers = summed_even, summed_odd
    for n in range(DATES // 2 + 1):
        if n < DATES // 2:
            columns_of_two(2 * n, buffers[n % 2])
        if n > 0:
            sum_lines(2 * n - 2, buffers[(n - 1) % 2])

    def first_step(n, carry):
        for u in range(UNROLL):
            column_entry(n * UNROLL + u)
        return carry

    def column_entry(k):
        offset = (reference + DATES - k) % DATES
        plain = (offset < PAIRS) | ((offset == PAIRS) & (k < reference))
        slot = jnp.where(plain, jnp.maximum(offset, 1), DATES - offset) - 1
        date = jnp.where(plain, k, reference)
        sign = jnp.where(offset == 0, 0.0, jnp.where(plain, 1.0, -1.0)).astype(F32)
        for g in range(half // TILE):
            real = jnp.where(offset == 0, diag[g, k], cov[g, slot, date, 0].astype(F32))
            imag = cov[g, slot, date, 1].astype(F32) * sign
            vec[g, k, 0] = real
            vec[g, k, 1] = imag
            narrow[g, k, 0] = real.astype(BF16)
            narrow[g, k, 1] = imag.astype(BF16)

    lax.fori_loop(0, DATES // UNROLL, first_step, 0)

    def one_tile(g, carry):
        def step(last):
            real = [packed(narrow[g, k, 0]) for k in range(DATES)]
            imag = [packed(narrow[g, k, 1]) for k in range(DATES)]
            for i in range(DATES):
                own = diag[g, i]
                total = [own * vec[g, i, 0], own * vec[g, i, 1]]
                sums = [None, None]
                others = [j for j in range(DATES) if j != i]
                for at in range(0, len(others), GROUP):
                    terms = [], []
                    for j in others[at : at + GROUP]:
                        slot, date, conjugated = entry(i, j)
                        a = packed(cov[g, slot, date, 0])
                        b = packed(cov[g, slot, date, 1])
                        if conjugated:
                            terms[0].append(a * real[j] + b * imag[j])
                            terms[1].append(a * imag[j] - b * real[j])
                        else:
                            terms[0].append(a * real[j] - b * imag[j])
                            terms[1].append(a * imag[j] + b * real[j])
                    for part in range(2):
                        term = tree(terms[part])
                        if last:
                            total[part] = total[part] + term.astype(F32)
                        else:
                            sums[part] = term if at == 0 else sums[part] + term
                for part in range(2):
                    if not last:
                        total[part] = total[part] + sums[part].astype(F32)
                        narrow[g, i, part] = total[part].astype(BF16)
                    vec[g, i, part] = total[part]

        def early_step(t, carry):
            step(False)
            return carry

        lax.fori_loop(0, POWER_ITERS - 2, early_step, 0)
        step(True)

        left_half = iota((TILE, lanes), 1) < ROWS
        squares = []
        for k in range(DATES):
            real, imag = vec[g, k, 0], vec[g, k, 1]
            squares.append(real * real + imag * imag)
        scale = DATES / tree(squares)
        ref_real = vec[g, reference, 0] * scale
        ref_imag = vec[g, reference, 1] * scale
        for k in range(DATES):
            real, imag = vec[g, k, 0], vec[g, k, 1]
            linked_real = (real * ref_real + imag * ref_imag).astype(BF16)
            linked_imag = (imag * ref_real - real * ref_imag).astype(BF16)
            linked_ref[g, k, 0] = jnp.where(
                left_half, linked_real, pltpu.roll(linked_imag, ROWS, 1)
            )
            linked_ref[g, k, 1] = jnp.where(
                left_half, pltpu.roll(linked_real, ROWS, 1), linked_imag
            )
        tile_out(g).start()
        return carry

    def tile_out(g):
        rows = pl.ds(pl.multiple_of(g * TILE, TILE), TILE)
        return pltpu.make_async_copy(
            linked_ref.at[g], linked_hbm.at[:, :, rows, :], sems.at[g]
        )

    lax.fori_loop(0, half // TILE, one_tile, 0)

    for g in range(half // TILE):
        tile_out(g).wait()


def link(z, reference, strip_columns):
    width = z.shape[1] - 2 * MARGIN
    half = width // 2
    tall = half + 2 * MARGIN
    lanes = 2 * ROWS
    return pl.pallas_call(
        functools.partial(link_kernel, strip_columns),
        out_shape=jax.ShapeDtypeStruct((DATES, 2, half, lanes), BF16),
        in_specs=[
            pl.BlockSpec(memory_space=pltpu.SMEM),
            pl.BlockSpec(memory_space=pltpu.VMEM),
        ],
        out_specs=pl.BlockSpec(memory_space=pltpu.HBM),
        scratch_shapes=[
            pltpu.VMEM((half // TILE, DATES, 2, TILE, lanes), BF16),
            pltpu.SemaphoreType.DMA((half // TILE,)),
            pltpu.VMEM((DATES, 2, tall, lanes), BF16),
            pltpu.VMEM((2, 2 * (PAIRS + 1) * half, lanes), BF16),
            pltpu.VMEM((2, 2 * (PAIRS + 1) * half, lanes), BF16),
            pltpu.VMEM((half // TILE, PAIRS, DATES, 2, TILE, lanes), BF16),
            pltpu.VMEM((half // TILE, DATES, TILE, lanes), F32),
            pltpu.VMEM((half // TILE, DATES, 2, TILE, lanes), F32),
            pltpu.VMEM((half // TILE, DATES, 2, TILE, lanes), BF16),
        ],
        cost_estimate=pl.CostEstimate(
            flops=16 * DATES * DATES * POWER_ITERS * width * ROWS,
            bytes_accessed=6 * DATES * width * ROWS,
            transcendentals=0,
        ),
        name="link",
    )(reference, *in_vmem(z))


def compress_kernel(linked_ref, z_ref, out_ref):
    dates, width, lanes = linked_ref.shape
    low = iota((width, lanes), 1) < ROWS

    def one_date(k, sums):
        linked = linked_ref[k].astype(F32)
        z = z_ref[k, MARGIN : MARGIN + width, :].astype(F32)
        return sums[0] + linked * z, sums[1] + linked * pltpu.roll(z, ROWS, 1)

    zero = jnp.zeros((width, lanes), F32)
    straight, crossed = lax.fori_loop(0, dates, one_date, (zero, zero))
    real = straight + pltpu.roll(straight, ROWS, 1)
    imag = pltpu.roll(crossed, ROWS, 1) - crossed
    turned = (jnp.where(low, real, imag) * (1.0 / math.sqrt(dates))).T
    out_ref[0] = turned[0:ROWS]
    out_ref[1] = turned[ROWS:]


def compress(linked, z):
    linked = linked.reshape(linked.shape[0], -1, 2 * ROWS)
    return pl.pallas_call(
        compress_kernel,
        out_shape=jax.ShapeDtypeStruct((2, ROWS, linked.shape[1]), F32),
        in_specs=[pl.BlockSpec(memory_space=pltpu.VMEM)] * 2,
        out_specs=pl.BlockSpec(memory_space=pltpu.VMEM),
        name="compress",
    )(linked, z)


def dct_table(line_count):
    frequency = jnp.arange(line_count, dtype=F32)[:, None]
    position = jnp.arange(line_count, dtype=F32)[None, :]
    weight = jnp.where(frequency == 0, math.sqrt(1.0 / line_count), math.sqrt(2.0 / line_count))
    return weight * jnp.cos(jnp.pi * (2.0 * position + 1.0) * frequency / (2.0 * line_count))


def dct_kernel(table_ref, x_ref, out_hbm, out_ref, sems):
    sources, width, lanes = x_ref.shape
    high, rest = split2(table_ref[...])
    zero = jnp.zeros_like(high)
    left = jnp.concatenate(
        [
            jnp.concatenate([high, zero, rest, zero], axis=1),
            jnp.concatenate([zero, high, zero, rest], axis=1),
        ],
        axis=0,
    )
    steps = sems.shape[0]
    each = sources // steps

    def columns_out(step):
        at = slice(step * each * width, (step + 1) * each * width)
        return pltpu.make_async_copy(
            out_ref.at[:, :, at], out_hbm.at[:, :, at], sems.at[step]
        )

    for source in range(0, sources, 2):
        x = jnp.concatenate([x_ref[source], x_ref[source + 1]], axis=0)
        result = lax.dot_general(
            left,
            jnp.concatenate([x, x], axis=1),
            (((1,), (1,)), ((), ())),
            preferred_element_type=F32,
        )
        columns = slice(source * width, (source + 2) * width)
        out_ref[0, :, columns] = result[0:ROWS]
        out_ref[1, :, columns] = result[ROWS:]
        if (source + 2) % each == 0:
            columns_out((source + 2) // each - 1).start()
    for step in range(steps):
        columns_out(step).wait()


def transform(linked):
    sources, width, _ = linked.shape
    shape = (2, ROWS, sources * width)
    return pl.pallas_call(
        dct_kernel,
        out_shape=jax.ShapeDtypeStruct(shape, F32),
        in_specs=[pl.BlockSpec(memory_space=pltpu.VMEM)] * 2,
        out_specs=pl.BlockSpec(memory_space=pltpu.HBM),
        scratch_shapes=[
            pltpu.VMEM(shape, F32),
            pltpu.SemaphoreType.DMA((math.gcd(sources // 2, STEPS),)),
        ],
        name="transform",
    )(*in_vmem(dct_table(ROWS), linked))


def exchange(blocks):
    return lax.all_to_all(blocks, "pix", split_axis=0, concat_axis=0, tiled=True)


def whole_dates(slcs, reference, strip_columns):
    arrived = exchange(pack(slcs, lax.axis_size("pix")))
    linked = link(arrived, reference, strip_columns)
    compressed = compress(linked, arrived)
    arrived = exchange(linked)
    return transform(arrived.reshape(arrived.shape[0], -1, 2 * ROWS)), compressed


def parts_of_dates(slcs, reference, strip_columns):
    devices = lax.axis_size("pix")
    width = strip_columns // devices
    local_rows = slcs.shape[1]
    padded = jnp.pad(slcs, ((0, 0), (0, 0), (MARGIN, MARGIN)))
    blocks = jnp.stack(
        [padded[:, :, d * width : d * width + width + 2 * MARGIN] for d in range(devices)]
    )
    window = exchange(blocks)
    per_date = ROWS // local_rows
    window = window.reshape(DATES, per_date, 2, local_rows, width + 2 * MARGIN)
    z = window.transpose(0, 4, 2, 1, 3).reshape(DATES, width + 2 * MARGIN, 2 * ROWS)
    linked = link(z, reference, strip_columns)
    compressed = compress(linked, z)
    linked = linked.astype(F32).reshape(DATES, width, 2, ROWS)
    spectrum = jnp.einsum(
        "qr,kcpr->kqpc", dct_table(ROWS), linked, precision=lax.Precision.HIGHEST
    ).reshape(DATES * ROWS // local_rows, local_rows, 2, width)
    arrived = exchange(spectrum.astype(BF16))
    spectrum = arrived.transpose(2, 1, 0, 3).reshape(2, local_rows, strip_columns)
    return spectrum.astype(F32), compressed


def on_device(slcs, ref_date):
    plan = whole_dates if slcs.shape[1] == ROWS else parts_of_dates
    return plan(slcs, ref_date, slcs.shape[2])


def solution(mesh):
    return jax.shard_map(
        on_device,
        mesh=mesh,
        in_specs=(P(None, ("grp", "pix"), None), P("grp")),
        out_specs=(P(None, ("grp", "pix"), None), P(None, None, ("grp", "pix"))),
        check_vma=False,
    )
```

```python
import functools
import math

import jax
import jax.numpy as jnp
from jax import lax
from jax.experimental import pallas as pl
from jax.experimental.pallas import tpu as pltpu
from jax.sharding import PartitionSpec as P

DATES = 16
ROWS = 64
HALF_X = 5
HALF_Y = 2
POWER_ITERS = 6
LOADING = 0.25

STEPS = 4
MARGIN = 8
TILE = 16
UNROLL = 4
GROUP = 4
PAIRS = DATES // 2
F32 = jnp.float32
BF16 = jnp.bfloat16


def iota(shape, dim):
    return lax.broadcasted_iota(jnp.int32, shape, dim)


def in_vmem(*arrays):
    return [pltpu.with_memory_space_constraint(x, pltpu.VMEM) for x in arrays]


def pack_kernel(x_hbm, out_hbm, x_ref, out_ref, in_sems, out_sems):
    devices, tall, _ = out_ref.shape
    width = tall - 2 * MARGIN
    steps = in_sems.shape[0]
    each = devices // steps

    def columns_in(step):
        at = slice(step * each * width, (step + 1) * each * width)
        return pltpu.make_async_copy(
            x_hbm.at[:, :, at], x_ref.at[:, :, at], in_sems.at[step]
        )

    def blocks_out(step):
        at = slice(step * each, (step + 1) * each)
        return pltpu.make_async_copy(out_ref.at[at], out_hbm.at[at], out_sems.at[step])

    for step in range(steps):
        columns_in(step).start()
    zero = jnp.zeros((MARGIN, out_ref.shape[2]), BF16)
    out_ref[0, 0:MARGIN, :] = zero
    out_ref[devices - 1, tall - MARGIN :, :] = zero
    for block in range(devices):
        if block % each == 0:
            columns_in(block // each).wait()
        columns = slice(block * width, (block + 1) * width)
        tile = jnp.concatenate([x_ref[0, :, columns], x_ref[1, :, columns]], axis=0)
        turned = tile.T
        out_ref[block, MARGIN : width + MARGIN, :] = turned
        if block > 0:
            out_ref[block - 1, width + MARGIN :, :] = turned[0:MARGIN]
        if block < devices - 1:
            out_ref[block + 1, 0:MARGIN, :] = turned[width - MARGIN :]
        if block % each == 0 and block > 0:
            blocks_out(block // each - 1).start()
    blocks_out(steps - 1).start()
    for step in range(steps):
        blocks_out(step).wait()


def pack(slcs, devices):
    parts, lines, columns = slcs.shape
    shape = (devices, columns // devices + 2 * MARGIN, parts * lines)
    steps = math.gcd(devices, STEPS)
    return pl.pallas_call(
        pack_kernel,
        out_shape=jax.ShapeDtypeStruct(shape, BF16),
        in_specs=[pl.BlockSpec(memory_space=pltpu.HBM)],
        out_specs=pl.BlockSpec(memory_space=pltpu.HBM),
        scratch_shapes=[
            pltpu.VMEM(slcs.shape, BF16),
            pltpu.VMEM(shape, BF16),
            pltpu.SemaphoreType.DMA((steps,)),
            pltpu.SemaphoreType.DMA((steps,)),
        ],
        name="pack",
    )(slcs)


def split2(x):
    high = x.astype(BF16)
    return high, (x - high.astype(F32)).astype(BF16)


def inverse_counts(first_column, strip_columns, half):
    shape = (half, 2 * ROWS)
    lane = iota(shape, 1)
    line = lane % ROWS
    column = first_column + iota(shape, 0) + (lane // ROWS) * half
    lines = jnp.minimum(line + HALF_Y, ROWS - 1) - jnp.maximum(line - HALF_Y, 0) + 1
    columns = (
        jnp.minimum(column + HALF_X, strip_columns - 1) - jnp.maximum(column - HALF_X, 0) + 1
    )
    return 1.0 / (lines * columns).astype(F32)


def tree(terms):
    while len(terms) > 1:
        terms = [
            terms[k] + terms[k + 1] if k + 1 < len(terms) else terms[k]
            for k in range(0, len(terms), 2)
        ]
    return terms[0]


def entry(i, j):
    offset = (j - i) % DATES
    if offset < PAIRS or (offset == PAIRS and i < j):
        return offset - 1, i, False
    return DATES - offset - 1, j, True


def packed(x):
    return x.astype(F32).astype(BF16)


def link_kernel(
    strip_columns,
    reference_ref,
    z_ref,
    linked_hbm,
    linked_ref,
    sems,
    window,
    summed_even,
    summed_odd,
    cov,
    diag,
    vec,
    narrow,
):
    tall = window.shape[2]
    half = tall - 2 * MARGIN
    lanes = 2 * ROWS
    reference = reference_ref[0]
    first_column = lax.axis_index("pix") * (strip_columns // lax.axis_size("pix"))

    low = iota((tall, lanes), 1) < ROWS

    unmixed = set()

    def unmix(k):
        if k in unmixed:
            return
        unmixed.add(k)
        top = packed(z_ref[k, 0:tall, :])
        bottom = packed(z_ref[k, half : half + tall, :])
        window[k, 0] = jnp.where(low, top, pltpu.roll(bottom, ROWS, 1))
        window[k, 1] = jnp.where(low, pltpu.roll(top, ROWS, 1), bottom)

    wide = 2 * lanes
    row, col = iota((wide, wide), 0), iota((wide, wide), 1)
    band_lines = jnp.where(
        (row // ROWS == col // ROWS) & (jnp.abs(row - col) <= HALF_Y), 1.0, 0.0
    ).astype(BF16)
    out_row, in_row = iota((half, tall), 0), iota((half, tall), 1)
    band_columns = jnp.where(jnp.abs(out_row + MARGIN - in_row) <= HALF_X, 1.0, 0.0).astype(BF16)
    inverse = inverse_counts(first_column, strip_columns, half)

    def offsets(i):
        return range(1, PAIRS + 1 if i < PAIRS else PAIRS)

    def sum_columns(i, slot, summed):
        unmix(i)
        real, imag = packed(window[i, 0]), packed(window[i, 1])
        real32, imag32 = real.astype(F32), imag.astype(F32)
        for offset in (0, *offsets(i)):
            if offset:
                j = (i + offset) % DATES
                unmix(j)
                real_j, imag_j = packed(window[j, 0]), packed(window[j, 1])
                left = real * real_j + imag * imag_j
                right = imag * real_j - real * imag_j
            else:
                left, right = split2(real32 * real32 + imag32 * imag32)
            sums = jnp.dot(
                band_columns,
                jnp.concatenate([left, right], axis=1),
                preferred_element_type=F32,
            )
            left, right = sums[:, 0:lanes], sums[:, lanes:]
            if offset:
                left, right = left.astype(BF16), right.astype(BF16)
            else:
                left, right = split2(left + right)
            at = (slot * len((0, *offsets(i))) + offset) * half
            summed[0, at : at + half] = left
            summed[1, at : at + half] = right

    def sum_lines(i, summed):
        count = len((0, *offsets(i)))
        used = slice(0, 2 * count * half)
        both = jnp.concatenate([packed(summed[0, used]), packed(summed[1, used])], axis=1)
        boxes = jnp.dot(both, band_lines, preferred_element_type=F32)
        for slot in range(2):
            for offset in (0, *offsets(i)):
                at = (slot * count + offset) * half
                box = boxes[at : at + half]
                if offset:
                    for part in range(2):
                        value = box[:, part * lanes : (part + 1) * lanes] * inverse
                        value = value.astype(BF16)
                        for g in range(half // TILE):
                            tile = value[g * TILE : (g + 1) * TILE]
                            cov[g, offset - 1, i + slot, part] = tile
                else:
                    value = (box[:, 0:lanes] + box[:, lanes:]) * inverse
                    value = value.astype(BF16).astype(F32) + LOADING
                    for g in range(half // TILE):
                        diag[g, i + slot] = value[g * TILE : (g + 1) * TILE]

    def columns_of_two(i, summed):
        for slot in range(2):
            sum_columns(i + slot, slot, summed)

    buffers = summed_even, summed_odd
    for n in range(DATES // 2 + 1):
        if n < DATES // 2:
            columns_of_two(2 * n, buffers[n % 2])
        if n > 0:
            sum_lines(2 * n - 2, buffers[(n - 1) % 2])

    def first_step(n, carry):
        for u in range(UNROLL):
            column_entry(n * UNROLL + u)
        return carry

    def column_entry(k):
        offset = (reference + DATES - k) % DATES
        plain = (offset < PAIRS) | ((offset == PAIRS) & (k < reference))
        slot = jnp.where(plain, jnp.maximum(offset, 1), DATES - offset) - 1
        date = jnp.where(plain, k, reference)
        sign = jnp.where(offset == 0, 0.0, jnp.where(plain, 1.0, -1.0)).astype(F32)
        for g in range(half // TILE):
            real = jnp.where(offset == 0, diag[g, k], cov[g, slot, date, 0].astype(F32))
            imag = cov[g, slot, date, 1].astype(F32) * sign
            vec[g, k, 0] = real
            vec[g, k, 1] = imag
            narrow[g, k, 0] = real.astype(BF16)
            narrow[g, k, 1] = imag.astype(BF16)

    lax.fori_loop(0, DATES // UNROLL, first_step, 0)

    def two_tiles(n, carry):
        tiles = 2 * n, 2 * n + 1

        def step(g, last):
            real = [packed(narrow[g, k, 0]) for k in range(DATES)]
            imag = [packed(narrow[g, k, 1]) for k in range(DATES)]
            for i in range(DATES):
                own = diag[g, i]
                total = [own * vec[g, i, 0], own * vec[g, i, 1]]
                sums = [None, None]
                others = [j for j in range(DATES) if j != i]
                for at in range(0, len(others), GROUP):
                    terms = [], []
                    for j in others[at : at + GROUP]:
                        slot, date, conjugated = entry(i, j)
                        a = packed(cov[g, slot, date, 0])
                        b = packed(cov[g, slot, date, 1])
                        if conjugated:
                            terms[0].append(a * real[j] + b * imag[j])
                            terms[1].append(a * imag[j] - b * real[j])
                        else:
                            terms[0].append(a * real[j] - b * imag[j])
                            terms[1].append(a * imag[j] + b * real[j])
                    for part in range(2):
                        term = tree(terms[part])
                        if last:
                            total[part] = total[part] + term.astype(F32)
                        else:
                            sums[part] = term if at == 0 else sums[part] + term
                for part in range(2):
                    if not last:
                        total[part] = total[part] + sums[part].astype(F32)
                        narrow[g, i, part] = total[part].astype(BF16)
                    vec[g, i, part] = total[part]

        def early_step(t, carry):
            for g in tiles:
                step(g, False)
            return carry

        lax.fori_loop(0, POWER_ITERS - 2, early_step, 0)
        for g in tiles:
            step(g, True)

            left_half = iota((TILE, lanes), 1) < ROWS
            squares = []
            for k in range(DATES):
                real, imag = vec[g, k, 0], vec[g, k, 1]
                squares.append(real * real + imag * imag)
            scale = DATES / tree(squares)
            ref_real = vec[g, reference, 0] * scale
            ref_imag = vec[g, reference, 1] * scale
            for k in range(DATES):
                real, imag = vec[g, k, 0], vec[g, k, 1]
                linked_real = (real * ref_real + imag * ref_imag).astype(BF16)
                linked_imag = (imag * ref_real - real * ref_imag).astype(BF16)
                linked_ref[g, k, 0] = jnp.where(
                    left_half, linked_real, pltpu.roll(linked_imag, ROWS, 1)
                )
                linked_ref[g, k, 1] = jnp.where(
                    left_half, pltpu.roll(linked_real, ROWS, 1), linked_imag
                )
            tile_out(g).start()
        return carry

    def tile_out(g):
        rows = pl.ds(pl.multiple_of(g * TILE, TILE), TILE)
        return pltpu.make_async_copy(
            linked_ref.at[g], linked_hbm.at[:, :, rows, :], sems.at[g]
        )

    lax.fori_loop(0, half // TILE // 2, two_tiles, 0)

    for g in range(half // TILE):
        tile_out(g).wait()


def link(z, reference, strip_columns):
    width = z.shape[1] - 2 * MARGIN
    half = width // 2
    tall = half + 2 * MARGIN
    lanes = 2 * ROWS
    return pl.pallas_call(
        functools.partial(link_kernel, strip_columns),
        out_shape=jax.ShapeDtypeStruct((DATES, 2, half, lanes), BF16),
        in_specs=[
            pl.BlockSpec(memory_space=pltpu.SMEM),
            pl.BlockSpec(memory_space=pltpu.VMEM),
        ],
        out_specs=pl.BlockSpec(memory_space=pltpu.HBM),
        scratch_shapes=[
            pltpu.VMEM((half // TILE, DATES, 2, TILE, lanes), BF16),
            pltpu.SemaphoreType.DMA((half // TILE,)),
            pltpu.VMEM((DATES, 2, tall, lanes), BF16),
            pltpu.VMEM((2, 2 * (PAIRS + 1) * half, lanes), BF16),
            pltpu.VMEM((2, 2 * (PAIRS + 1) * half, lanes), BF16),
            pltpu.VMEM((half // TILE, PAIRS, DATES, 2, TILE, lanes), BF16),
            pltpu.VMEM((half // TILE, DATES, TILE, lanes), F32),
            pltpu.VMEM((half // TILE, DATES, 2, TILE, lanes), F32),
            pltpu.VMEM((half // TILE, DATES, 2, TILE, lanes), BF16),
        ],
        cost_estimate=pl.CostEstimate(
            flops=16 * DATES * DATES * POWER_ITERS * width * ROWS,
            bytes_accessed=6 * DATES * width * ROWS,
            transcendentals=0,
        ),
        name="link",
    )(reference, *in_vmem(z))


def compress_kernel(linked_ref, z_ref, out_ref):
    dates, width, lanes = linked_ref.shape
    low = iota((width, lanes), 1) < ROWS

    def one_date(k, sums):
        linked = linked_ref[k].astype(F32)
        z = z_ref[k, MARGIN : MARGIN + width, :].astype(F32)
        return sums[0] + linked * z, sums[1] + linked * pltpu.roll(z, ROWS, 1)

    zero = jnp.zeros((width, lanes), F32)
    straight, crossed = lax.fori_loop(0, dates, one_date, (zero, zero))
    real = straight + pltpu.roll(straight, ROWS, 1)
    imag = pltpu.roll(crossed, ROWS, 1) - crossed
    turned = (jnp.where(low, real, imag) * (1.0 / math.sqrt(dates))).T
    out_ref[0] = turned[0:ROWS]
    out_ref[1] = turned[ROWS:]


def compress(linked, z):
    linked = linked.reshape(linked.shape[0], -1, 2 * ROWS)
    return pl.pallas_call(
        compress_kernel,
        out_shape=jax.ShapeDtypeStruct((2, ROWS, linked.shape[1]), F32),
        in_specs=[pl.BlockSpec(memory_space=pltpu.VMEM)] * 2,
        out_specs=pl.BlockSpec(memory_space=pltpu.VMEM),
        name="compress",
    )(linked, z)


def dct_table(line_count):
    frequency = jnp.arange(line_count, dtype=F32)[:, None]
    position = jnp.arange(line_count, dtype=F32)[None, :]
    weight = jnp.where(frequency == 0, math.sqrt(1.0 / line_count), math.sqrt(2.0 / line_count))
    return weight * jnp.cos(jnp.pi * (2.0 * position + 1.0) * frequency / (2.0 * line_count))


def dct_kernel(table_ref, x_ref, out_hbm, out_ref, sems):
    sources, width, lanes = x_ref.shape
    high, rest = split2(table_ref[...])
    zero = jnp.zeros_like(high)
    left = jnp.concatenate(
        [
            jnp.concatenate([high, zero, rest, zero], axis=1),
            jnp.concatenate([zero, high, zero, rest], axis=1),
        ],
        axis=0,
    )
    steps = sems.shape[0]
    each = sources // steps

    def columns_out(step):
        at = slice(step * each * width, (step + 1) * each * width)
        return pltpu.make_async_copy(
            out_ref.at[:, :, at], out_hbm.at[:, :, at], sems.at[step]
        )

    for source in range(0, sources, 2):
        x = jnp.concatenate([x_ref[source], x_ref[source + 1]], axis=0)
        result = lax.dot_general(
            left,
            jnp.concatenate([x, x], axis=1),
            (((1,), (1,)), ((), ())),
            preferred_element_type=F32,
        )
        columns = slice(source * width, (source + 2) * width)
        out_ref[0, :, columns] = result[0:ROWS]
        out_ref[1, :, columns] = result[ROWS:]
        if (source + 2) % each == 0:
            columns_out((source + 2) // each - 1).start()
    for step in range(steps):
        columns_out(step).wait()


def transform(linked):
    sources, width, _ = linked.shape
    shape = (2, ROWS, sources * width)
    return pl.pallas_call(
        dct_kernel,
        out_shape=jax.ShapeDtypeStruct(shape, F32),
        in_specs=[pl.BlockSpec(memory_space=pltpu.VMEM)] * 2,
        out_specs=pl.BlockSpec(memory_space=pltpu.HBM),
        scratch_shapes=[
            pltpu.VMEM(shape, F32),
            pltpu.SemaphoreType.DMA((math.gcd(sources // 2, STEPS),)),
        ],
        name="transform",
    )(*in_vmem(dct_table(ROWS), linked))


def exchange(blocks):
    return lax.all_to_all(blocks, "pix", split_axis=0, concat_axis=0, tiled=True)


def whole_dates(slcs, reference, strip_columns):
    arrived = exchange(pack(slcs, lax.axis_size("pix")))
    linked = link(arrived, reference, strip_columns)
    compressed = compress(linked, arrived)
    arrived = exchange(linked)
    return transform(arrived.reshape(arrived.shape[0], -1, 2 * ROWS)), compressed


def parts_of_dates(slcs, reference, strip_columns):
    devices = lax.axis_size("pix")
    width = strip_columns // devices
    local_rows = slcs.shape[1]
    padded = jnp.pad(slcs, ((0, 0), (0, 0), (MARGIN, MARGIN)))
    blocks = jnp.stack(
        [padded[:, :, d * width : d * width + width + 2 * MARGIN] for d in range(devices)]
    )
    window = exchange(blocks)
    per_date = ROWS // local_rows
    window = window.reshape(DATES, per_date, 2, local_rows, width + 2 * MARGIN)
    z = window.transpose(0, 4, 2, 1, 3).reshape(DATES, width + 2 * MARGIN, 2 * ROWS)
    linked = link(z, reference, strip_columns)
    compressed = compress(linked, z)
    linked = linked.astype(F32).reshape(DATES, width, 2, ROWS)
    spectrum = jnp.einsum(
        "qr,kcpr->kqpc", dct_table(ROWS), linked, precision=lax.Precision.HIGHEST
    ).reshape(DATES * ROWS // local_rows, local_rows, 2, width)
    arrived = exchange(spectrum.astype(BF16))
    spectrum = arrived.transpose(2, 1, 0, 3).reshape(2, local_rows, strip_columns)
    return spectrum.astype(F32), compressed


def on_device(slcs, ref_date):
    plan = whole_dates if slcs.shape[1] == ROWS else parts_of_dates
    return plan(slcs, ref_date, slcs.shape[2])


def solution(mesh):
    return jax.shard_map(
        on_device,
        mesh=mesh,
        in_specs=(P(None, ("grp", "pix"), None), P("grp")),
        out_specs=(P(None, ("grp", "pix"), None), P(None, None, ("grp", "pix"))),
        check_vma=False,
    )
```

```python
import functools
import math

import jax
import jax.numpy as jnp
from jax import lax
from jax.experimental import pallas as pl
from jax.experimental.pallas import tpu as pltpu
from jax.sharding import PartitionSpec as P

DATES = 16
ROWS = 64
HALF_X = 5
HALF_Y = 2
POWER_ITERS = 6
LOADING = 0.25

STEPS = 4
MARGIN = 8
TILE = 16
UNROLL = 4
GROUP = 4
PAIRS = DATES // 2
F32 = jnp.float32
BF16 = jnp.bfloat16


def iota(shape, dim):
    return lax.broadcasted_iota(jnp.int32, shape, dim)


def in_vmem(*arrays):
    return [pltpu.with_memory_space_constraint(x, pltpu.VMEM) for x in arrays]


def pack_kernel(x_hbm, out_hbm, x_ref, out_ref, in_sems, out_sems):
    devices, tall, _ = out_ref.shape
    width = tall - 2 * MARGIN
    steps = in_sems.shape[0]
    each = devices // steps

    def columns_in(step):
        at = slice(step * each * width, (step + 1) * each * width)
        return pltpu.make_async_copy(
            x_hbm.at[:, :, at], x_ref.at[:, :, at], in_sems.at[step]
        )

    def blocks_out(step):
        at = slice(step * each, (step + 1) * each)
        return pltpu.make_async_copy(out_ref.at[at], out_hbm.at[at], out_sems.at[step])

    for step in range(steps):
        columns_in(step).start()
    zero = jnp.zeros((MARGIN, out_ref.shape[2]), BF16)
    out_ref[0, 0:MARGIN, :] = zero
    out_ref[devices - 1, tall - MARGIN :, :] = zero
    for block in range(devices):
        if block % each == 0:
            columns_in(block // each).wait()
        columns = slice(block * width, (block + 1) * width)
        tile = jnp.concatenate([x_ref[0, :, columns], x_ref[1, :, columns]], axis=0)
        turned = tile.T
        out_ref[block, MARGIN : width + MARGIN, :] = turned
        if block > 0:
            out_ref[block - 1, width + MARGIN :, :] = turned[0:MARGIN]
        if block < devices - 1:
            out_ref[block + 1, 0:MARGIN, :] = turned[width - MARGIN :]
        if block % each == 0 and block > 0:
            blocks_out(block // each - 1).start()
    blocks_out(steps - 1).start()
    for step in range(steps):
        blocks_out(step).wait()


def pack(slcs, devices):
    parts, lines, columns = slcs.shape
    shape = (devices, columns // devices + 2 * MARGIN, parts * lines)
    steps = math.gcd(devices, STEPS // 2)
    return pl.pallas_call(
        pack_kernel,
        out_shape=jax.ShapeDtypeStruct(shape, BF16),
        in_specs=[pl.BlockSpec(memory_space=pltpu.HBM)],
        out_specs=pl.BlockSpec(memory_space=pltpu.HBM),
        scratch_shapes=[
            pltpu.VMEM(slcs.shape, BF16),
            pltpu.VMEM(shape, BF16),
            pltpu.SemaphoreType.DMA((steps,)),
            pltpu.SemaphoreType.DMA((steps,)),
        ],
        name="pack",
    )(slcs)


def split2(x):
    high = x.astype(BF16)
    return high, (x - high.astype(F32)).astype(BF16)


def inverse_counts(first_column, strip_columns, half):
    shape = (half, 2 * ROWS)
    lane = iota(shape, 1)
    line = lane % ROWS
    column = first_column + iota(shape, 0) + (lane // ROWS) * half
    lines = jnp.minimum(line + HALF_Y, ROWS - 1) - jnp.maximum(line - HALF_Y, 0) + 1
    columns = (
        jnp.minimum(column + HALF_X, strip_columns - 1) - jnp.maximum(column - HALF_X, 0) + 1
    )
    return 1.0 / (lines * columns).astype(F32)


def tree(terms):
    while len(terms) > 1:
        terms = [
            terms[k] + terms[k + 1] if k + 1 < len(terms) else terms[k]
            for k in range(0, len(terms), 2)
        ]
    return terms[0]


def entry(i, j):
    offset = (j - i) % DATES
    if offset < PAIRS or (offset == PAIRS and i < j):
        return offset - 1, i, False
    return DATES - offset - 1, j, True


def packed(x):
    return x.astype(F32).astype(BF16)


def link_kernel(
    strip_columns,
    reference_ref,
    z_ref,
    linked_hbm,
    linked_ref,
    sems,
    window,
    summed_even,
    summed_odd,
    cov,
    diag,
    vec,
    narrow,
):
    tall = window.shape[2]
    half = tall - 2 * MARGIN
    lanes = 2 * ROWS
    reference = reference_ref[0]
    first_column = lax.axis_index("pix") * (strip_columns // lax.axis_size("pix"))

    low = iota((tall, lanes), 1) < ROWS

    unmixed = set()

    def unmix(k):
        if k in unmixed:
            return
        unmixed.add(k)
        top = packed(z_ref[k, 0:tall, :])
        bottom = packed(z_ref[k, half : half + tall, :])
        window[k, 0] = jnp.where(low, top, pltpu.roll(bottom, ROWS, 1))
        window[k, 1] = jnp.where(low, pltpu.roll(top, ROWS, 1), bottom)

    wide = 2 * lanes
    row, col = iota((wide, wide), 0), iota((wide, wide), 1)
    band_lines = jnp.where(
        (row // ROWS == col // ROWS) & (jnp.abs(row - col) <= HALF_Y), 1.0, 0.0
    ).astype(BF16)
    out_row, in_row = iota((half, tall), 0), iota((half, tall), 1)
    band_columns = jnp.where(jnp.abs(out_row + MARGIN - in_row) <= HALF_X, 1.0, 0.0).astype(BF16)
    inverse = inverse_counts(first_column, strip_columns, half)

    def offsets(i):
        return range(1, PAIRS + 1 if i < PAIRS else PAIRS)

    def sum_columns(i, slot, summed):
        unmix(i)
        real, imag = packed(window[i, 0]), packed(window[i, 1])
        real32, imag32 = real.astype(F32), imag.astype(F32)
        for offset in (0, *offsets(i)):
            if offset:
                j = (i + offset) % DATES
                unmix(j)
                real_j, imag_j = packed(window[j, 0]), packed(window[j, 1])
                left = real * real_j + imag * imag_j
                right = imag * real_j - real * imag_j
            else:
                left, right = split2(real32 * real32 + imag32 * imag32)
            sums = jnp.dot(
                band_columns,
                jnp.concatenate([left, right], axis=1),
                preferred_element_type=F32,
            )
            left, right = sums[:, 0:lanes], sums[:, lanes:]
            if offset:
                left, right = left.astype(BF16), right.astype(BF16)
            else:
                left, right = split2(left + right)
            at = (slot * len((0, *offsets(i))) + offset) * half
            summed[0, at : at + half] = left
            summed[1, at : at + half] = right

    def sum_lines(i, summed):
        count = len((0, *offsets(i)))
        used = slice(0, 2 * count * half)
        both = jnp.concatenate([packed(summed[0, used]), packed(summed[1, used])], axis=1)
        boxes = jnp.dot(both, band_lines, preferred_element_type=F32)
        for slot in range(2):
            for offset in (0, *offsets(i)):
                at = (slot * count + offset) * half
                box = boxes[at : at + half]
                if offset:
                    for part in range(2):
                        value = box[:, part * lanes : (part + 1) * lanes] * inverse
                        value = value.astype(BF16)
                        for g in range(half // TILE):
                            tile = value[g * TILE : (g + 1) * TILE]
                            cov[g, offset - 1, i + slot, part] = tile
                else:
                    value = (box[:, 0:lanes] + box[:, lanes:]) * inverse
                    value = value.astype(BF16).astype(F32) + LOADING
                    for g in range(half // TILE):
                        diag[g, i + slot] = value[g * TILE : (g + 1) * TILE]

    def columns_of_two(i, summed):
        for slot in range(2):
            sum_columns(i + slot, slot, summed)

    buffers = summed_even, summed_odd
    for n in range(DATES // 2 + 1):
        if n < DATES // 2:
            columns_of_two(2 * n, buffers[n % 2])
        if n > 0:
            sum_lines(2 * n - 2, buffers[(n - 1) % 2])

    def first_step(n, carry):
        for u in range(UNROLL):
            column_entry(n * UNROLL + u)
        return carry

    def column_entry(k):
        offset = (reference + DATES - k) % DATES
        plain = (offset < PAIRS) | ((offset == PAIRS) & (k < reference))
        slot = jnp.where(plain, jnp.maximum(offset, 1), DATES - offset) - 1
        date = jnp.where(plain, k, reference)
        sign = jnp.where(offset == 0, 0.0, jnp.where(plain, 1.0, -1.0)).astype(F32)
        for g in range(half // TILE):
            real = jnp.where(offset == 0, diag[g, k], cov[g, slot, date, 0].astype(F32))
            imag = cov[g, slot, date, 1].astype(F32) * sign
            vec[g, k, 0] = real
            vec[g, k, 1] = imag
            narrow[g, k, 0] = real.astype(BF16)
            narrow[g, k, 1] = imag.astype(BF16)

    lax.fori_loop(0, DATES // UNROLL, first_step, 0)

    def one_tile(g, carry):
        def step(last):
            real = [packed(narrow[g, k, 0]) for k in range(DATES)]
            imag = [packed(narrow[g, k, 1]) for k in range(DATES)]
            for i in range(DATES):
                own = diag[g, i]
                total = [own * vec[g, i, 0], own * vec[g, i, 1]]
                sums = [None, None]
                others = [j for j in range(DATES) if j != i]
                for at in range(0, len(others), GROUP):
                    terms = [], []
                    for j in others[at : at + GROUP]:
                        slot, date, conjugated = entry(i, j)
                        a = packed(cov[g, slot, date, 0])
                        b = packed(cov[g, slot, date, 1])
                        if conjugated:
                            terms[0].append(a * real[j] + b * imag[j])
                            terms[1].append(a * imag[j] - b * real[j])
                        else:
                            terms[0].append(a * real[j] - b * imag[j])
                            terms[1].append(a * imag[j] + b * real[j])
                    for part in range(2):
                        term = tree(terms[part])
                        if last:
                            total[part] = total[part] + term.astype(F32)
                        else:
                            sums[part] = term if at == 0 else sums[part] + term
                for part in range(2):
                    if not last:
                        total[part] = total[part] + sums[part].astype(F32)
                        narrow[g, i, part] = total[part].astype(BF16)
                    vec[g, i, part] = total[part]

        def early_step(t, carry):
            step(False)
            return carry

        lax.fori_loop(0, POWER_ITERS - 2, early_step, 0)
        step(True)

        left_half = iota((TILE, lanes), 1) < ROWS
        squares = []
        for k in range(DATES):
            real, imag = vec[g, k, 0], vec[g, k, 1]
            squares.append(real * real + imag * imag)
        scale = DATES / tree(squares)
        ref_real = vec[g, reference, 0] * scale
        ref_imag = vec[g, reference, 1] * scale
        for k in range(DATES):
            real, imag = vec[g, k, 0], vec[g, k, 1]
            linked_real = (real * ref_real + imag * ref_imag).astype(BF16)
            linked_imag = (imag * ref_real - real * ref_imag).astype(BF16)
            linked_ref[g, k, 0] = jnp.where(
                left_half, linked_real, pltpu.roll(linked_imag, ROWS, 1)
            )
            linked_ref[g, k, 1] = jnp.where(
                left_half, pltpu.roll(linked_real, ROWS, 1), linked_imag
            )
        tile_out(g).start()
        return carry

    def tile_out(g):
        rows = pl.ds(pl.multiple_of(g * TILE, TILE), TILE)
        return pltpu.make_async_copy(
            linked_ref.at[g], linked_hbm.at[:, :, rows, :], sems.at[g]
        )

    lax.fori_loop(0, half // TILE, one_tile, 0)

    for g in range(half // TILE):
        tile_out(g).wait()


def link(z, reference, strip_columns):
    width = z.shape[1] - 2 * MARGIN
    half = width // 2
    tall = half + 2 * MARGIN
    lanes = 2 * ROWS
    return pl.pallas_call(
        functools.partial(link_kernel, strip_columns),
        out_shape=jax.ShapeDtypeStruct((DATES, 2, half, lanes), BF16),
        in_specs=[
            pl.BlockSpec(memory_space=pltpu.SMEM),
            pl.BlockSpec(memory_space=pltpu.VMEM),
        ],
        out_specs=pl.BlockSpec(memory_space=pltpu.HBM),
        scratch_shapes=[
            pltpu.VMEM((half // TILE, DATES, 2, TILE, lanes), BF16),
            pltpu.SemaphoreType.DMA((half // TILE,)),
            pltpu.VMEM((DATES, 2, tall, lanes), BF16),
            pltpu.VMEM((2, 2 * (PAIRS + 1) * half, lanes), BF16),
            pltpu.VMEM((2, 2 * (PAIRS + 1) * half, lanes), BF16),
            pltpu.VMEM((half // TILE, PAIRS, DATES, 2, TILE, lanes), BF16),
            pltpu.VMEM((half // TILE, DATES, TILE, lanes), F32),
            pltpu.VMEM((half // TILE, DATES, 2, TILE, lanes), F32),
            pltpu.VMEM((half // TILE, DATES, 2, TILE, lanes), BF16),
        ],
        cost_estimate=pl.CostEstimate(
            flops=16 * DATES * DATES * POWER_ITERS * width * ROWS,
            bytes_accessed=6 * DATES * width * ROWS,
            transcendentals=0,
        ),
        name="link",
    )(reference, *in_vmem(z))


def compress_kernel(linked_ref, z_ref, out_ref):
    dates, width, lanes = linked_ref.shape
    low = iota((width, lanes), 1) < ROWS

    def one_date(k, sums):
        linked = linked_ref[k].astype(F32)
        z = z_ref[k, MARGIN : MARGIN + width, :].astype(F32)
        return sums[0] + linked * z, sums[1] + linked * pltpu.roll(z, ROWS, 1)

    zero = jnp.zeros((width, lanes), F32)
    straight, crossed = lax.fori_loop(0, dates, one_date, (zero, zero))
    real = straight + pltpu.roll(straight, ROWS, 1)
    imag = pltpu.roll(crossed, ROWS, 1) - crossed
    turned = (jnp.where(low, real, imag) * (1.0 / math.sqrt(dates))).T
    out_ref[0] = turned[0:ROWS]
    out_ref[1] = turned[ROWS:]


def compress(linked, z):
    linked = linked.reshape(linked.shape[0], -1, 2 * ROWS)
    return pl.pallas_call(
        compress_kernel,
        out_shape=jax.ShapeDtypeStruct((2, ROWS, linked.shape[1]), F32),
        in_specs=[pl.BlockSpec(memory_space=pltpu.VMEM)] * 2,
        out_specs=pl.BlockSpec(memory_space=pltpu.VMEM),
        name="compress",
    )(linked, z)


def dct_table(line_count):
    frequency = jnp.arange(line_count, dtype=F32)[:, None]
    position = jnp.arange(line_count, dtype=F32)[None, :]
    weight = jnp.where(frequency == 0, math.sqrt(1.0 / line_count), math.sqrt(2.0 / line_count))
    return weight * jnp.cos(jnp.pi * (2.0 * position + 1.0) * frequency / (2.0 * line_count))


def dct_kernel(table_ref, x_ref, out_hbm, out_ref, sems):
    sources, width, lanes = x_ref.shape
    high, rest = split2(table_ref[...])
    zero = jnp.zeros_like(high)
    left = jnp.concatenate(
        [
            jnp.concatenate([high, zero, rest, zero], axis=1),
            jnp.concatenate([zero, high, zero, rest], axis=1),
        ],
        axis=0,
    )
    steps = sems.shape[0]
    each = sources // steps

    def columns_out(step):
        at = slice(step * each * width, (step + 1) * each * width)
        return pltpu.make_async_copy(
            out_ref.at[:, :, at], out_hbm.at[:, :, at], sems.at[step]
        )

    for source in range(0, sources, 2):
        x = jnp.concatenate([x_ref[source], x_ref[source + 1]], axis=0)
        result = lax.dot_general(
            left,
            jnp.concatenate([x, x], axis=1),
            (((1,), (1,)), ((), ())),
            preferred_element_type=F32,
        )
        columns = slice(source * width, (source + 2) * width)
        out_ref[0, :, columns] = result[0:ROWS]
        out_ref[1, :, columns] = result[ROWS:]
        if (source + 2) % each == 0:
            columns_out((source + 2) // each - 1).start()
    for step in range(steps):
        columns_out(step).wait()


def transform(linked):
    sources, width, _ = linked.shape
    shape = (2, ROWS, sources * width)
    return pl.pallas_call(
        dct_kernel,
        out_shape=jax.ShapeDtypeStruct(shape, F32),
        in_specs=[pl.BlockSpec(memory_space=pltpu.VMEM)] * 2,
        out_specs=pl.BlockSpec(memory_space=pltpu.HBM),
        scratch_shapes=[
            pltpu.VMEM(shape, F32),
            pltpu.SemaphoreType.DMA((math.gcd(sources // 2, STEPS),)),
        ],
        name="transform",
    )(*in_vmem(dct_table(ROWS), linked))


def exchange(blocks):
    return lax.all_to_all(blocks, "pix", split_axis=0, concat_axis=0, tiled=True)


def whole_dates(slcs, reference, strip_columns):
    arrived = exchange(pack(slcs, lax.axis_size("pix")))
    linked = link(arrived, reference, strip_columns)
    compressed = compress(linked, arrived)
    arrived = exchange(linked)
    return transform(arrived.reshape(arrived.shape[0], -1, 2 * ROWS)), compressed


def parts_of_dates(slcs, reference, strip_columns):
    devices = lax.axis_size("pix")
    width = strip_columns // devices
    local_rows = slcs.shape[1]
    padded = jnp.pad(slcs, ((0, 0), (0, 0), (MARGIN, MARGIN)))
    blocks = jnp.stack(
        [padded[:, :, d * width : d * width + width + 2 * MARGIN] for d in range(devices)]
    )
    window = exchange(blocks)
    per_date = ROWS // local_rows
    window = window.reshape(DATES, per_date, 2, local_rows, width + 2 * MARGIN)
    z = window.transpose(0, 4, 2, 1, 3).reshape(DATES, width + 2 * MARGIN, 2 * ROWS)
    linked = link(z, reference, strip_columns)
    compressed = compress(linked, z)
    linked = linked.astype(F32).reshape(DATES, width, 2, ROWS)
    spectrum = jnp.einsum(
        "qr,kcpr->kqpc", dct_table(ROWS), linked, precision=lax.Precision.HIGHEST
    ).reshape(DATES * ROWS // local_rows, local_rows, 2, width)
    arrived = exchange(spectrum.astype(BF16))
    spectrum = arrived.transpose(2, 1, 0, 3).reshape(2, local_rows, strip_columns)
    return spectrum.astype(F32), compressed


def on_device(slcs, ref_date):
    plan = whole_dates if slcs.shape[1] == ROWS else parts_of_dates
    return plan(slcs, ref_date, slcs.shape[2])


def solution(mesh):
    return jax.shard_map(
        on_device,
        mesh=mesh,
        in_specs=(P(None, ("grp", "pix"), None), P("grp")),
        out_specs=(P(None, ("grp", "pix"), None), P(None, None, ("grp", "pix"))),
        check_vma=False,
    )
```
